128 devices in a mesh: tm: 8 (over z_hi, x), space: 16 (over y, z_lo, core).
Axes of the slice: x: 4, y: 4, z: 4 (z_hi: 2, z_lo: 2; z = z_hi * 2 + z_lo), core: 2. Of those that a mesh axis runs over, the one named last changes fastest.
Arguments:
- courant: float32 [64, 256, 256], P('space'), may hold values from 0.04 to 0.3
- misfit: float32 [64, 256, 256], P('space'), may hold values from -6 to 6
- wavelet: float32 [128], P('tm'), may hold values from -1.5 to 1.5
- source_cells: int32 [128], P('tm'), may hold values from 0 to 4194303
- boundary_states: float32 [8, 2, 64, 256, 256], P('tm', None, 'space'), may hold values from -6 to 6
Outputs:
- updated_states: float32 [8, 2, 64, 256, 256], P('tm', None, 'space')
- source_gradient: float32 [128], P('tm')
The draws below stay inside these ranges and needn't reach their ends.
Inputs may be any that keep to these rules, and one draw needn't show every extreme that they name: `source_cells`: each entry is a flattened cell index x * 256 * 256 + y * 256 + z of the fine grid.
All inputs are finite; a program needn't handle non-finite values.
Results may differ from the reference program's by a relative error of at most 0.0001.
Values sent between devices are 32-bit elements; how exact they have to be, the bound alone decides.
No kernel may reach another device: no remote copies, remote signals or barrier semaphores. Data moves between devices by JAX's collectives and lax.ppermute only.
A program may use at most 192 MiB of HBM per device.

```python
import math
import jax
import jax.numpy as jnp

NY = 256
NZ = 256
STEPS = 16
COARSE = 8
NX = 64
GROUPS = 8
TOTAL = 128
N_TM = 8


def touch_ends(entries, own_key, low, largest):
    dims = entries.shape
    spot = [jax.random.randint(jax.random.fold_in(own_key, axis), (), 0, dims[axis]) for axis in range(len(dims))]
    entries = entries.at[tuple(spot)].set(low)
    longest = dims.index(max(dims))
    spot[longest] = (spot[longest] + 1) % dims[longest]
    return entries.at[tuple(spot)].set(largest)


def levels(own_key, extent, cuts, smallest, largest):
    def one(axis_at, blocks):
        steps = jax.random.uniform(jax.random.fold_in(jax.random.fold_in(own_key, 6), axis_at), (blocks,), jnp.float32, smallest / len(cuts), largest / len(cuts))
        return jnp.repeat(jnp.exp(steps), extent[axis_at] // blocks).reshape((-1,) + (1,) * (len(extent) - axis_at - 1))

    factor_of = one(*cuts[0])
    for cut in cuts[1:]:
        factor_of = factor_of * one(*cut)
    return factor_of


def scatter_about(rng, shape, spread, limit, pieces=(), dtype=jnp.bfloat16):
    array = spread * jax.random.normal(rng, shape, jnp.float32)
    if pieces:
        array = array * levels(rng, shape, pieces, -0.22, 0.18)
    return jnp.clip(array, -limit, limit).astype(dtype)


def setup_inputs(seed: int = 0) -> dict:
    splits = jax.random.split(jax.random.key(seed), 6)
    courant = jnp.clip(jnp.exp(math.log(0.3) - 2.014903 * jax.random.uniform(splits[0], (NX, NY, NZ), jnp.float32) ** levels(splits[0], (NX, NY, NZ), ((0, 16),), -0.2, 0.2)), 0.04, 0.3)
    misfit = scatter_about(splits[1], (NX, NY, NZ), 1.0, 6.0, ((0, 16),), jnp.float32)
    wavelet = scatter_about(splits[2], (TOTAL,), 0.3, 1.5, ((0, 8),), jnp.float32)
    source_cells = touch_ends(jax.random.randint(splits[3], (TOTAL,), 0, NX * NY * NZ), jax.random.fold_in(splits[3], 1), 0, (NX * NY * NZ) - 1).astype(jnp.int32)
    boundary_states = scatter_about(splits[4], (GROUPS, 2, NX, NY, NZ), 1.0, 6.0, ((0, 8), (2, 16)), jnp.float32)
    return {"courant": courant, "misfit": misfit, "wavelet": wavelet, "source_cells": source_cells, "boundary_states": boundary_states}


def laplace(field):
    padded = jnp.pad(field, 1)
    beside = padded[2:, 1:-1, 1:-1] + padded[:-2, 1:-1, 1:-1]
    beside = beside + padded[1:-1, 2:, 1:-1] + padded[1:-1, :-2, 1:-1]
    beside = beside + padded[1:-1, 1:-1, 2:] + padded[1:-1, 1:-1, :-2]
    return beside - 6.0 * field


def restrict(field):
    a, b, c = field.shape
    return field.reshape(a // 2, 2, b // 2, 2, c // 2, 2).mean(axis=(1, 3, 5))


def prolong(field):
    return jnp.repeat(jnp.repeat(jnp.repeat(field, 2, axis=0), 2, axis=1), 2, axis=2)


def coarse_map(first, second, coarse_courant):
    for turn in range(COARSE):
        earlier = 2.0 * first - second + coarse_courant * laplace(first)
        second = first
        first = earlier
    return first, second


def reference(courant, misfit, wavelet, source_cells, boundary_states):
    groups = N_TM
    samples = [None] * (groups * STEPS)
    restricted = []
    for group in range(groups):
        if group + 1 < groups:
            current = boundary_states[group + 1, 0]
            following = boundary_states[group + 1, 1]
        else:
            current = jnp.zeros_like(courant)
            following = jnp.zeros_like(courant)
        for level in reversed(range(group * STEPS, (group + 1) * STEPS)):
            earlier = 2.0 * current - following + courant * laplace(current) + wavelet[level] * misfit
            samples[level] = earlier.reshape(-1)[source_cells[level]]
            following = current
            current = earlier
        resid_first = current - boundary_states[group, 0]
        resid_second = following - boundary_states[group, 1]
        restricted.append((restrict(resid_first), restrict(resid_second)))
    coarse_courant = restrict(courant)
    first = jnp.zeros_like(restricted[0][0])
    second = jnp.zeros_like(restricted[0][0])
    updated = [None] * groups
    for group in reversed(range(groups)):
        first, second = coarse_map(first, second, coarse_courant)
        first = first + restricted[group][0]
        second = second + restricted[group][1]
        updated[group] = jnp.stack((boundary_states[group, 0] + prolong(first), boundary_states[group, 1] + prolong(second)))
    return jnp.stack(updated), jnp.stack(samples)
```

```python
import functools

import jax
import jax.numpy as jnp
from jax import lax
from jax.experimental import pallas as pl
from jax.experimental.pallas import tpu as pltpu
from jax.sharding import PartitionSpec as P

COARSE = 8
GROUPS = 8
SLABS = 16
ROWS = 32
HIGH = lax.Precision.HIGHEST

SNAKE = tuple(
    y * 4 + z * 2 + c for y in range(4) for z in ((0, 1) if y % 2 == 0 else (1, 0)) for c in (0, 1)
)
PLACE = tuple(SNAKE.index(s) for s in range(SLABS))
VM = pl.BlockSpec(memory_space=pltpu.VMEM)
SM = pl.BlockSpec(memory_space=pltpu.SMEM)


def exchange(block, order, offset):
    pairs = []
    for i in range(offset, SLABS - 1, 2):
        pairs += [(order[i], order[i + 1]), (order[i + 1], order[i])]
    return lax.ppermute(block, "space", pairs)


def call(kernel, out_shapes, args, specs, scratch=(), aliases=None, cost=None):
    return pl.pallas_call(
        kernel,
        out_shape=out_shapes,
        in_specs=specs,
        out_specs=jax.tree.map(lambda _: VM, out_shapes),
        scratch_shapes=list(scratch),
        input_output_aliases=aliases or {},
        cost_estimate=cost,
    )(*args)


def f32(*shape):
    return jax.ShapeDtypeStruct(shape, jnp.float32)


def halving(rows, cols):
    r = lax.broadcasted_iota(jnp.int32, (rows, cols), 0)
    c = lax.broadcasted_iota(jnp.int32, (rows, cols), 1)
    if rows < cols:
        return jnp.where(c // 2 == r, 1.0, 0.0).astype(jnp.float32)
    return jnp.where(r // 2 == c, 1.0, 0.0).astype(jnp.float32)


def dot(a, b):
    return jnp.dot(a, b, precision=HIGH, preferred_element_type=jnp.float32)


def restrict_plane(pair_sum):
    ny, nz = pair_sum.shape
    part = dot(pair_sum, halving(nz, nz // 2))
    return dot(halving(ny // 2, ny), part) * 0.125


def update_plane(mid, lower, upper, before, speed, force, weight, out):
    ny, nz = mid.shape
    lane = lax.broadcasted_iota(jnp.int32, (ROWS, nz), 1)
    row = lax.broadcasted_iota(jnp.int32, (ROWS, nz), 0)
    for r0 in range(0, ny, ROWS):
        here = slice(r0, r0 + ROWS)
        m = mid[here, :]
        if r0 == 0:
            up = jnp.where(row == 0, 0.0, pltpu.roll(m, 1, 0))
        else:
            up = mid[r0 - 1 : r0 - 1 + ROWS, :]
        if r0 + ROWS == ny:
            down = jnp.where(row == ROWS - 1, 0.0, pltpu.roll(m, ROWS - 1, 0))
        else:
            down = mid[r0 + 1 : r0 + 1 + ROWS, :]
        left = jnp.where(lane == 0, 0.0, pltpu.roll(m, 1, 1))
        right = jnp.where(lane == nz - 1, 0.0, pltpu.roll(m, nz - 1, 1))
        beside = (lower[here, :] + upper[here, :]) + (up + down) + (left + right)
        out[here, :] = (
            2.0 * m - before[here, :] + speed[here, :] * (beside - 6.0 * m) + weight * force[here, :]
        )


def sampled_row(planes, info, cell):
    ny, nz = planes[0].shape
    x = cell // (ny * nz) - info[1] * len(planes)
    y = lax.rem(cell // nz, ny)
    z = lax.rem(cell, nz)
    q = jnp.where(info[0] == 1, len(planes) - 1 - x, x)
    lane = lax.broadcasted_iota(jnp.int32, (1, nz), 1)
    row = jnp.zeros((1, nz), jnp.float32)
    for k, plane in enumerate(planes):
        row = jnp.where((lane == z) & (q == k), plane[pl.ds(y, 1), :], row)
    return row


def prep_kernel(info, courant, misfit, states, ce, ci, fe, fi, e0, e1, inner, b0, b1, binner, rb, rc):
    odd = info[0] == 1
    alive = (info[2] == 1).astype(jnp.float32)
    for xc in range(2):
        rc[xc] = restrict_plane(courant[2 * xc] + courant[2 * xc + 1])
        for lev in range(2):
            rb[lev, xc] = restrict_plane(states[lev, 2 * xc] + states[lev, 2 * xc + 1])

    def spread(flip):
        q = (lambda k: 3 - k) if flip else (lambda k: k)
        ce[0], ce[1] = courant[q(0)], courant[q(3)]
        ci[0], ci[1] = courant[q(1)], courant[q(2)]
        fe[0], fe[1] = misfit[q(0)], misfit[q(3)]
        fi[0], fi[1] = misfit[q(1)], misfit[q(2)]
        e0[...] = states[0, q(0)] * alive
        e1[...] = states[0, q(3)] * alive
        inner[0], inner[1] = states[0, q(1)] * alive, states[0, q(2)] * alive
        b0[...] = states[1, q(0)] * alive
        b1[...] = states[1, q(3)] * alive
        binner[0], binner[1] = states[1, q(1)] * alive, states[1, q(2)] * alive

    @pl.when(odd)
    def _():
        spread(True)

    @pl.when(jnp.logical_not(odd))
    def _():
        spread(False)


def edge_kernel(level, taken, info, cells, wavelet, e0, e1, inner, b0, b1, off, on, ce, fe, samples, n0, n1, out_samples):
    weight = wavelet[level]
    update_plane(e0, off, inner.at[0], b0, ce.at[0], fe.at[0], weight, n0)
    update_plane(e1, inner.at[1], on, b1, ce.at[1], fe.at[1], weight, n1)
    out_samples[...] = samples[...]
    if taken is not None:
        planes = (e0, inner.at[0], inner.at[1], e1)
        out_samples[taken : taken + 1, :] = sampled_row(planes, info, cells[taken])


def inner_kernel(level, wavelet, e0, e1, inner, before, ci, fi, out):
    weight = wavelet[level]
    update_plane(inner.at[0], e0, inner.at[1], before.at[0], ci.at[0], fi.at[0], weight, out.at[0])
    update_plane(inner.at[1], inner.at[0], e1, before.at[1], ci.at[1], fi.at[1], weight, out.at[1])


def leave_kernel(info, cells, e0, e1, inner, b0, b1, binner, samples, rb, rc, out):
    odd = info[0] == 1
    block = out.shape[2]
    for lev, (first, last, mid) in enumerate(((e0, e1, inner), (b0, b1, binner))):
        low = first[...] + mid[0]
        high = last[...] + mid[1]
        for xc, total in enumerate((jnp.where(odd, high, low), jnp.where(odd, low, high))):
            r = restrict_plane(total) - rb[lev, xc]
            for s in range(SLABS):
                out[s, lev * 2 + xc] = r[PLACE[s] * block : (PLACE[s] + 1) * block, :]
    for xc in range(2):
        for s in range(SLABS):
            out[s, 4 + xc] = rc[xc, PLACE[s] * block : (PLACE[s] + 1) * block, :]
    row = sampled_row((e0, inner.at[0], inner.at[1], e1), info, cells[0])
    count = samples.shape[0]
    at = lax.broadcasted_iota(jnp.int32, (count, 1), 0)
    values = jnp.where(at == 0, jnp.sum(row), jnp.sum(samples[...], axis=1, keepdims=True))
    lane = lax.broadcasted_iota(jnp.int32, (count, 128), 1)
    level = lax.broadcasted_iota(jnp.int32, (count, 128), 0)
    line = jnp.sum(jnp.where(lane == level, values, 0.0), axis=0, keepdims=True)
    for s in range(SLABS):
        out[s, 6] = jnp.broadcast_to(line, (block, 128))


def phi_kernel(has_add, info, state, on, off, speed, son, soff, *rest):
    if has_add:
        add, out, a, b, c = rest
    else:
        out, a, b, c = rest
    odd = info[0] == 1
    nx = speed.shape[0] * speed.shape[1]
    block = speed.shape[2]
    tall, nz = 3 * block, 128
    zero = jnp.zeros((tall, nz), jnp.float32)
    a[0], a[nx + 1], b[0], b[nx + 1] = zero, zero, zero, zero

    def fill(above, below, sabove, sbelow):
        for k, (rows, source, ssource) in enumerate(
            ((slice(0, block), above, sabove), (slice(block, 2 * block), state, speed), (slice(2 * block, tall), below, sbelow))
        ):
            a[1 : nx + 1, rows, :] = source[:, 0:2].reshape(nx, block, nz)
            b[1 : nx + 1, rows, :] = source[:, 2:4].reshape(nx, block, nz)
            c[:, rows, :] = ssource[...].reshape(nx, block, nz)

    @pl.when(odd)
    def _():
        fill(on, off, son, soff)

    @pl.when(jnp.logical_not(odd))
    def _():
        fill(off, on, soff, son)

    step_x = 4
    lane = lax.broadcasted_iota(jnp.int32, (step_x, tall, nz), 2)

    def turn(now, then):
        for x0 in range(0, nx, step_x):
            m = now[x0 + 1 : x0 + 1 + step_x]
            beside = now[x0 : x0 + step_x] + now[x0 + 2 : x0 + 2 + step_x]
            beside = beside + pltpu.roll(m, 1, 1) + pltpu.roll(m, tall - 1, 1)
            beside = beside + jnp.where(lane == 0, 0.0, pltpu.roll(m, 1, 2))
            beside = beside + jnp.where(lane == nz - 1, 0.0, pltpu.roll(m, nz - 1, 2))
            then[x0 + 1 : x0 + 1 + step_x] = (
                2.0 * m - then[x0 + 1 : x0 + 1 + step_x] + c[x0 : x0 + step_x] * (beside - 6.0 * m)
            )

    def two(_, carry):
        turn(a, b)
        turn(b, a)
        return carry

    lax.fori_loop(0, COARSE // 2, two, 0)
    rows = slice(block, 2 * block)
    one = a[1 : nx + 1, rows, :].reshape(SLABS, 2, block, nz)
    other = b[1 : nx + 1, rows, :].reshape(SLABS, 2, block, nz)
    if has_add:
        one = one + add[:, 0:2]
        other = other + add[:, 2:4]
    out[:, 0:2] = one
    out[:, 2:4] = other


def arrive_kernel(coarse, states, out, plane):
    block = coarse.shape[2]
    nyc, nzc = plane.shape
    for lev in range(2):
        for xc in range(2):
            for s in range(SLABS):
                plane[PLACE[s] * block : (PLACE[s] + 1) * block, :] = coarse[s, lev * 2 + xc]
            fine = dot(dot(halving(2 * nyc, nyc), plane[...]), halving(nzc, 2 * nzc))
            out[lev, 2 * xc] = states[lev, 2 * xc] + fine
            out[lev, 2 * xc + 1] = states[lev, 2 * xc + 1] + fine


def body(courant, misfit, wavelet, source_cells, boundary_states):
    steps = wavelet.shape[0]
    ny, nz = courant.shape[1:]
    nyc, nzc = ny // 2, nz // 2
    block = nyc // SLABS
    slab = lax.axis_index("space")
    tm = lax.axis_index("tm")
    states = boundary_states[0]
    natural = tuple(range(SLABS))
    odd = lax.rem(slab, 2)
    alive = (tm > 0).astype(jnp.int32)
    info = jnp.stack([odd, slab, alive]).astype(jnp.int32)
    ring = [(i, (i + 1) % GROUPS) for i in range(GROUPS)]

    mask = alive.astype(jnp.float32)
    first_off = lax.dynamic_index_in_dim(states[0], 3 * odd, 0, keepdims=False) * mask
    first_on = lax.dynamic_index_in_dim(states[0], 3 - 3 * odd, 0, keepdims=False) * mask
    on = exchange(first_on, natural, 0)
    off = exchange(first_off, natural, 1)
    packed = jnp.stack([wavelet, source_cells.astype(jnp.float32)])
    packed = lax.ppermute(packed, "tm", ring)
    weights = packed[0]
    cells = packed[1].astype(jnp.int32)

    plane2 = f32(2, ny, nz)
    plane = f32(ny, nz)
    ce, ci, fe, fi, e0, e1, inner, b0, b1, binner, rb, rc = call(
        prep_kernel,
        (plane2,) * 4 + (plane, plane, plane2) * 2 + (f32(2, 2, nyc, nzc), f32(2, nyc, nzc)),
        (info, courant, misfit, states),
        [SM, VM, VM, VM],
    )
    rb = lax.ppermute(rb, "tm", ring)
    samples = jnp.zeros((steps, nz), jnp.float32)
    for turn in range(steps):
        level = steps - 1 - turn
        n0, n1, samples = call(
            functools.partial(edge_kernel, level, level + 1 if turn else None),
            (plane, plane, f32(steps, nz)),
            (info, cells, weights, e0, e1, inner, b0, b1, off, on, ce, fe, samples),
            [SM, SM, SM] + [VM] * 10,
        )
        if turn < steps - 1:
            on = exchange(n1, natural, 0)
            off = exchange(n0, natural, 1)
        ninner = call(
            functools.partial(inner_kernel, level),
            plane2,
            (weights, e0, e1, inner, binner, ci, fi),
            [SM] + [VM] * 6,
        )
        e0, e1, inner, b0, b1, binner = n0, n1, ninner, e0, e1, inner

    pieces = call(
        leave_kernel,
        f32(SLABS, 7, block, nzc),
        (info, cells, e0, e1, inner, b0, b1, binner, samples, rb, rc),
        [SM, SM] + [VM] * 9,
    )
    pieces = lax.all_to_all(pieces, "space", 0, 0)
    total = pieces[:, :4]
    speed = pieces[:, 4:6]
    son = exchange(speed, SNAKE, 0)
    soff = exchange(speed, SNAKE, 1)
    line = jnp.sum(pieces[:, 6, 0, :], axis=0)

    def phi(state, add=None):
        sides = (exchange(state, SNAKE, 0), exchange(state, SNAKE, 1))
        nx = SLABS * 2
        args = (info, state, *sides, speed, son, soff) + (() if add is None else (add,))
        return call(
            functools.partial(phi_kernel, add is not None),
            f32(SLABS, 4, block, nzc),
            args,
            [SM] + [VM] * (len(args) - 1),
            scratch=[pltpu.VMEM((nx + 2, 3 * block, nzc), jnp.float32)] * 2
            + [pltpu.VMEM((nx, 3 * block, nzc), jnp.float32)],
        )

    def later(state, distance, aligned):
        route = []
        for to in range(GROUPS):
            group = to if aligned else (to - 1) % GROUPS
            if group + distance < GROUPS:
                route.append(((group + distance + 1) % GROUPS, to))
        return lax.ppermute(state, "tm", route)

    total = phi(later(total, 1, False), total)
    total = phi(phi(later(total, 2, False)), total)
    moved = later(total, 4, True)
    back = [(i, (i - 1) % GROUPS) for i in range(GROUPS)]
    own = lax.ppermute(total, "tm", back)
    gradient = lax.ppermute(line, "tm", back)[:steps]
    for turn in range(4):
        moved = phi(moved, own if turn == 3 else None)
    coarse = lax.all_to_all(moved, "space", 0, 0)
    updated = call(
        arrive_kernel,
        f32(2, 4, ny, nz),
        (coarse, states),
        [VM, VM],
        scratch=[pltpu.VMEM((nyc, nzc), jnp.float32)],
    )
    return (updated[None], gradient)


def solution(mesh):
    placed = (
        P("space", None, None),
        P("space", None, None),
        P("tm"),
        P("tm"),
        P("tm", None, "space", None, None),
    )
    return jax.shard_map(
        body,
        mesh=mesh,
        in_specs=placed,
        out_specs=(P("tm", None, "space", None, None), P("tm")),
        check_vma=False,
    )
```

```python
import functools

import jax
import jax.numpy as jnp
from jax import lax
from jax.experimental import pallas as pl
from jax.experimental.pallas import tpu as pltpu
from jax.sharding import PartitionSpec as P

COARSE = 8
GROUPS = 8
SLABS = 16
ROWS = 32
HIGH = lax.Precision.HIGHEST

SNAKE = tuple(
    y * 4 + z * 2 + c for y in range(4) for z in ((0, 1) if y % 2 == 0 else (1, 0)) for c in (0, 1)
)
PLACE = tuple(SNAKE.index(s) for s in range(SLABS))
VM = pl.BlockSpec(memory_space=pltpu.VMEM)
SM = pl.BlockSpec(memory_space=pltpu.SMEM)


def exchange(block, order, offset):
    pairs = []
    for i in range(offset, SLABS - 1, 2):
        pairs += [(order[i], order[i + 1]), (order[i + 1], order[i])]
    return lax.ppermute(block, "space", pairs)


def call(kernel, out_shapes, args, specs, scratch=(), aliases=None, cost=None):
    return pl.pallas_call(
        kernel,
        out_shape=out_shapes,
        in_specs=specs,
        out_specs=jax.tree.map(lambda _: VM, out_shapes),
        scratch_shapes=list(scratch),
        input_output_aliases=aliases or {},
        cost_estimate=cost,
        compiler_params=pltpu.CompilerParams(vmem_limit_bytes=16 << 20),
    )(*args)


def f32(*shape):
    return jax.ShapeDtypeStruct(shape, jnp.float32)


def halving(rows, cols):
    r = lax.broadcasted_iota(jnp.int32, (rows, cols), 0)
    c = lax.broadcasted_iota(jnp.int32, (rows, cols), 1)
    if rows < cols:
        return jnp.where(c // 2 == r, 1.0, 0.0).astype(jnp.float32)
    return jnp.where(r // 2 == c, 1.0, 0.0).astype(jnp.float32)


def dot(a, b):
    return jnp.dot(a, b, precision=HIGH, preferred_element_type=jnp.float32)


def restrict_plane(pair_sum):
    ny, nz = pair_sum.shape
    part = dot(pair_sum, halving(nz, nz // 2))
    return dot(halving(ny // 2, ny), part) * 0.125


def update_plane(mid, lower, upper, before, speed, force, weight, out):
    ny, nz = mid.shape
    lane = lax.broadcasted_iota(jnp.int32, (ROWS, nz), 1)
    row = lax.broadcasted_iota(jnp.int32, (ROWS, nz), 0)
    for r0 in range(0, ny, ROWS):
        here = slice(r0, r0 + ROWS)
        m = mid[here, :]
        if r0 == 0:
            up = jnp.where(row == 0, 0.0, pltpu.roll(m, 1, 0))
        else:
            up = mid[r0 - 1 : r0 - 1 + ROWS, :]
        if r0 + ROWS == ny:
            down = jnp.where(row == ROWS - 1, 0.0, pltpu.roll(m, ROWS - 1, 0))
        else:
            down = mid[r0 + 1 : r0 + 1 + ROWS, :]
        left = jnp.where(lane == 0, 0.0, pltpu.roll(m, 1, 1))
        right = jnp.where(lane == nz - 1, 0.0, pltpu.roll(m, nz - 1, 1))
        beside = (lower[here, :] + upper[here, :]) + (up + down) + (left + right)
        out[here, :] = (
            2.0 * m - before[here, :] + speed[here, :] * (beside - 6.0 * m) + weight * force[here, :]
        )


def sampled_row(planes, info, cell):
    ny, nz = planes[0].shape
    x = cell // (ny * nz) - info[1] * len(planes)
    y = lax.rem(cell // nz, ny)
    z = lax.rem(cell, nz)
    q = jnp.where(info[0] == 1, len(planes) - 1 - x, x)
    lane = lax.broadcasted_iota(jnp.int32, (1, nz), 1)
    row = jnp.zeros((1, nz), jnp.float32)
    for k, plane in enumerate(planes):
        row = jnp.where((lane == z) & (q == k), plane[pl.ds(y, 1), :], row)
    return row


def prep_kernel(info, courant, misfit, states, ce, ci, fe, fi, e0, e1, inner, b0, b1, binner, rb, rc):
    odd = info[0] == 1
    alive = (info[2] == 1).astype(jnp.float32)
    for xc in range(2):
        rc[xc] = restrict_plane(courant[2 * xc] + courant[2 * xc + 1])
        for lev in range(2):
            rb[lev, xc] = restrict_plane(states[lev, 2 * xc] + states[lev, 2 * xc + 1])

    def spread(flip):
        q = (lambda k: 3 - k) if flip else (lambda k: k)
        ce[0], ce[1] = courant[q(0)], courant[q(3)]
        ci[0], ci[1] = courant[q(1)], courant[q(2)]
        fe[0], fe[1] = misfit[q(0)], misfit[q(3)]
        fi[0], fi[1] = misfit[q(1)], misfit[q(2)]
        e0[...] = states[0, q(0)] * alive
        e1[...] = states[0, q(3)] * alive
        inner[0], inner[1] = states[0, q(1)] * alive, states[0, q(2)] * alive
        b0[...] = states[1, q(0)] * alive
        b1[...] = states[1, q(3)] * alive
        binner[0], binner[1] = states[1, q(1)] * alive, states[1, q(2)] * alive

    @pl.when(odd)
    def _():
        spread(True)

    @pl.when(jnp.logical_not(odd))
    def _():
        spread(False)


def edge_kernel(level, taken, info, cells, wavelet, e0, e1, inner, b0, b1, off, on, ce, fe, samples, n0, n1, out_samples):
    weight = wavelet[level]
    update_plane(e0, off, inner.at[0], b0, ce.at[0], fe.at[0], weight, n0)
    update_plane(e1, inner.at[1], on, b1, ce.at[1], fe.at[1], weight, n1)
    out_samples[...] = samples[...]
    if taken is not None:
        planes = (e0, inner.at[0], inner.at[1], e1)
        out_samples[taken : taken + 1, :] = sampled_row(planes, info, cells[taken])


def inner_kernel(level, wavelet, e0, e1, inner, before, ci, fi, out):
    weight = wavelet[level]
    update_plane(inner.at[0], e0, inner.at[1], before.at[0], ci.at[0], fi.at[0], weight, out.at[0])
    update_plane(inner.at[1], inner.at[0], e1, before.at[1], ci.at[1], fi.at[1], weight, out.at[1])


def leave_kernel(info, cells, e0, e1, inner, b0, b1, binner, samples, rb, rc, out):
    odd = info[0] == 1
    block = out.shape[2]
    for lev, (first, last, mid) in enumerate(((e0, e1, inner), (b0, b1, binner))):
        low = first[...] + mid[0]
        high = last[...] + mid[1]
        for xc, total in enumerate((jnp.where(odd, high, low), jnp.where(odd, low, high))):
            r = restrict_plane(total) - rb[lev, xc]
            for s in range(SLABS):
                out[s, lev * 2 + xc] = r[PLACE[s] * block : (PLACE[s] + 1) * block, :]
    for xc in range(2):
        for s in range(SLABS):
            out[s, 4 + xc] = rc[xc, PLACE[s] * block : (PLACE[s] + 1) * block, :]
    row = sampled_row((e0, inner.at[0], inner.at[1], e1), info, cells[0])
    count = samples.shape[0]
    at = lax.broadcasted_iota(jnp.int32, (count, 1), 0)
    values = jnp.where(at == 0, jnp.sum(row), jnp.sum(samples[...], axis=1, keepdims=True))
    lane = lax.broadcasted_iota(jnp.int32, (count, 128), 1)
    level = lax.broadcasted_iota(jnp.int32, (count, 128), 0)
    line = jnp.sum(jnp.where(lane == level, values, 0.0), axis=0, keepdims=True)
    for s in range(SLABS):
        out[s, 6] = jnp.broadcast_to(line, (block, 128))


def phi_kernel(has_add, info, state, on, off, speed, son, soff, *rest):
    if has_add:
        add, out, a, b, c = rest
    else:
        out, a, b, c = rest
    odd = info[0] == 1
    nx = speed.shape[0] * speed.shape[1]
    block = speed.shape[2]
    tall, nz = 3 * block, 128
    zero = jnp.zeros((tall, nz), jnp.float32)
    a[0], a[nx + 1], b[0], b[nx + 1] = zero, zero, zero, zero

    def fill(above, below, sabove, sbelow):
        for k, (rows, source, ssource) in enumerate(
            ((slice(0, block), above, sabove), (slice(block, 2 * block), state, speed), (slice(2 * block, tall), below, sbelow))
        ):
            a[1 : nx + 1, rows, :] = source[:, 0:2].reshape(nx, block, nz)
            b[1 : nx + 1, rows, :] = source[:, 2:4].reshape(nx, block, nz)
            c[:, rows, :] = ssource[...].reshape(nx, block, nz)

    @pl.when(odd)
    def _():
        fill(on, off, son, soff)

    @pl.when(jnp.logical_not(odd))
    def _():
        fill(off, on, soff, son)

    step_x = 4
    lane = lax.broadcasted_iota(jnp.int32, (step_x, tall, nz), 2)

    def turn(now, then):
        for x0 in range(0, nx, step_x):
            m = now[x0 + 1 : x0 + 1 + step_x]
            beside = now[x0 : x0 + step_x] + now[x0 + 2 : x0 + 2 + step_x]
            beside = beside + pltpu.roll(m, 1, 1) + pltpu.roll(m, tall - 1, 1)
            beside = beside + jnp.where(lane == 0, 0.0, pltpu.roll(m, 1, 2))
            beside = beside + jnp.where(lane == nz - 1, 0.0, pltpu.roll(m, nz - 1, 2))
            then[x0 + 1 : x0 + 1 + step_x] = (
                2.0 * m - then[x0 + 1 : x0 + 1 + step_x] + c[x0 : x0 + step_x] * (beside - 6.0 * m)
            )

    def two(_, carry):
        turn(a, b)
        turn(b, a)
        return carry

    lax.fori_loop(0, COARSE // 2, two, 0)
    rows = slice(block, 2 * block)
    one = a[1 : nx + 1, rows, :].reshape(SLABS, 2, block, nz)
    other = b[1 : nx + 1, rows, :].reshape(SLABS, 2, block, nz)
    if has_add:
        one = one + add[:, 0:2]
        other = other + add[:, 2:4]
    out[:, 0:2] = one
    out[:, 2:4] = other


def arrive_kernel(coarse, states, out, plane):
    block = coarse.shape[2]
    nyc, nzc = plane.shape
    for lev in range(2):
        for xc in range(2):
            for s in range(SLABS):
                plane[PLACE[s] * block : (PLACE[s] + 1) * block, :] = coarse[s, lev * 2 + xc]
            fine = dot(dot(halving(2 * nyc, nyc), plane[...]), halving(nzc, 2 * nzc))
            out[lev, 2 * xc] = states[lev, 2 * xc] + fine
            out[lev, 2 * xc + 1] = states[lev, 2 * xc + 1] + fine


def body(courant, misfit, wavelet, source_cells, boundary_states):
    steps = wavelet.shape[0]
    ny, nz = courant.shape[1:]
    nyc, nzc = ny // 2, nz // 2
    block = nyc // SLABS
    slab = lax.axis_index("space")
    tm = lax.axis_index("tm")
    states = boundary_states[0]
    natural = tuple(range(SLABS))
    odd = lax.rem(slab, 2)
    alive = (tm > 0).astype(jnp.int32)
    info = jnp.stack([odd, slab, alive]).astype(jnp.int32)
    ring = [(i, (i + 1) % GROUPS) for i in range(GROUPS)]

    mask = alive.astype(jnp.float32)
    first_off = lax.dynamic_index_in_dim(states[0], 3 * odd, 0, keepdims=False) * mask
    first_on = lax.dynamic_index_in_dim(states[0], 3 - 3 * odd, 0, keepdims=False) * mask
    on = exchange(first_on, natural, 0)
    off = exchange(first_off, natural, 1)
    packed = jnp.stack([wavelet, source_cells.astype(jnp.float32)])
    packed = lax.ppermute(packed, "tm", ring)
    weights = packed[0]
    cells = packed[1].astype(jnp.int32)

    plane2 = f32(2, ny, nz)
    plane = f32(ny, nz)
    ce, ci, fe, fi, e0, e1, inner, b0, b1, binner, rb, rc = call(
        prep_kernel,
        (plane2,) * 4 + (plane, plane, plane2) * 2 + (f32(2, 2, nyc, nzc), f32(2, nyc, nzc)),
        (info, courant, misfit, states),
        [SM, VM, VM, VM],
    )
    rb = lax.ppermute(rb, "tm", ring)
    samples = jnp.zeros((steps, nz), jnp.float32)
    for turn in range(steps):
        level = steps - 1 - turn
        n0, n1, samples = call(
            functools.partial(edge_kernel, level, level + 1 if turn else None),
            (plane, plane, f32(steps, nz)),
            (info, cells, weights, e0, e1, inner, b0, b1, off, on, ce, fe, samples),
            [SM, SM, SM] + [VM] * 10,
        )
        if turn < steps - 1:
            on = exchange(n1, natural, 0)
            off = exchange(n0, natural, 1)
        ninner = call(
            functools.partial(inner_kernel, level),
            plane2,
            (weights, e0, e1, inner, binner, ci, fi),
            [SM] + [VM] * 6,
        )
        e0, e1, inner, b0, b1, binner = n0, n1, ninner, e0, e1, inner

    pieces = call(
        leave_kernel,
        f32(SLABS, 7, block, nzc),
        (info, cells, e0, e1, inner, b0, b1, binner, samples, rb, rc),
        [SM, SM] + [VM] * 9,
    )
    pieces = lax.all_to_all(pieces, "space", 0, 0)
    total = pieces[:, :4]
    speed = pieces[:, 4:6]
    son = exchange(speed, SNAKE, 0)
    soff = exchange(speed, SNAKE, 1)
    line = jnp.sum(pieces[:, 6, 0, :], axis=0)

    def phi(state, add=None):
        sides = (exchange(state, SNAKE, 0), exchange(state, SNAKE, 1))
        nx = SLABS * 2
        args = (info, state, *sides, speed, son, soff) + (() if add is None else (add,))
        return call(
            functools.partial(phi_kernel, add is not None),
            f32(SLABS, 4, block, nzc),
            args,
            [SM] + [VM] * (len(args) - 1),
            scratch=[pltpu.VMEM((nx + 2, 3 * block, nzc), jnp.float32)] * 2
            + [pltpu.VMEM((nx, 3 * block, nzc), jnp.float32)],
        )

    def later(state, distance, aligned):
        route = []
        for to in range(GROUPS):
            group = to if aligned else (to - 1) % GROUPS
            if group + distance < GROUPS:
                route.append(((group + distance + 1) % GROUPS, to))
        return lax.ppermute(state, "tm", route)

    total = phi(later(total, 1, False), total)
    total = phi(phi(later(total, 2, False)), total)
    moved = later(total, 4, True)
    back = [(i, (i - 1) % GROUPS) for i in range(GROUPS)]
    own = lax.ppermute(total, "tm", back)
    gradient = lax.ppermute(line, "tm", back)[:steps]
    for turn in range(4):
        moved = phi(moved, own if turn == 3 else None)
    coarse = lax.all_to_all(moved, "space", 0, 0)
    updated = call(
        arrive_kernel,
        f32(2, 4, ny, nz),
        (coarse, states),
        [VM, VM],
        scratch=[pltpu.VMEM((nyc, nzc), jnp.float32)],
    )
    return (updated[None], gradient)


def solution(mesh):
    placed = (
        P("space", None, None),
        P("space", None, None),
        P("tm"),
        P("tm"),
        P("tm", None, "space", None, None),
    )
    return jax.shard_map(
        body,
        mesh=mesh,
        in_specs=placed,
        out_specs=(P("tm", None, "space", None, None), P("tm")),
        check_vma=False,
    )
```

```python
import functools

import jax
import jax.numpy as jnp
from jax import lax
from jax.experimental import pallas as pl
from jax.experimental.pallas import tpu as pltpu
from jax.sharding import PartitionSpec as P

COARSE = 8
GROUPS = 8
SLABS = 16
ROWS = 32
UNROLL = 8
HIGH = lax.Precision.HIGHEST

SNAKE = tuple(
    y * 4 + z * 2 + c for y in range(4) for z in ((0, 1) if y % 2 == 0 else (1, 0)) for c in (0, 1)
)
PLACE = tuple(SNAKE.index(s) for s in range(SLABS))
VM = pl.BlockSpec(memory_space=pltpu.VMEM)
SM = pl.BlockSpec(memory_space=pltpu.SMEM)


def exchange(block, order, offset):
    pairs = []
    for i in range(offset, SLABS, 2):
        here, there = order[i], order[(i + 1) % SLABS]
        pairs += [(here, there), (there, here)]
    return lax.ppermute(block, "space", pairs)


def call(kernel, out_shapes, args, specs, scratch=(), aliases=None, cost=None):
    return pl.pallas_call(
        kernel,
        out_shape=out_shapes,
        in_specs=specs,
        out_specs=jax.tree.map(lambda _: VM, out_shapes),
        scratch_shapes=list(scratch),
        input_output_aliases=aliases or {},
        cost_estimate=cost,
        compiler_params=pltpu.CompilerParams(vmem_limit_bytes=16 << 20),
    )(*args)


def f32(*shape):
    return jax.ShapeDtypeStruct(shape, jnp.float32)


def halving(rows, cols):
    r = lax.broadcasted_iota(jnp.int32, (rows, cols), 0)
    c = lax.broadcasted_iota(jnp.int32, (rows, cols), 1)
    hit = c // 2 == r if rows < cols else r // 2 == c
    return jnp.where(hit, 1.0, 0.0).astype(jnp.bfloat16)


def dot(a, ones):
    total = None
    for _ in range(3):
        part = a.astype(jnp.bfloat16)
        a = a - part.astype(jnp.float32)
        term = jnp.dot(part, ones, preferred_element_type=jnp.float32)
        total = term if total is None else total + term
    return total


def restrict_planes(first, second, tall):
    ny, nz = first.shape
    tall[...] = dot(first[...] + second[...], halving(nz, nz // 2))
    half = ny // 2
    return (tall[pl.ds(0, half, stride=2), :] + tall[pl.ds(1, half, stride=2), :]) * 0.125


def update_plane(mid, lower, upper, before, speed, force, weight, out, reach=None):
    ny, nz = mid.shape
    lane = lax.broadcasted_iota(jnp.int32, (ROWS, nz), 1)
    row = lax.broadcasted_iota(jnp.int32, (ROWS, nz), 0)
    for r0 in range(0, ny, ROWS):
        here = slice(r0, r0 + ROWS)
        m = mid[here, :]
        if r0 == 0:
            up = jnp.where(row == 0, 0.0, pltpu.roll(m, 1, 0))
        else:
            up = mid[r0 - 1 : r0 - 1 + ROWS, :]
        if r0 + ROWS == ny:
            down = jnp.where(row == ROWS - 1, 0.0, pltpu.roll(m, ROWS - 1, 0))
        else:
            down = mid[r0 + 1 : r0 + 1 + ROWS, :]
        left = jnp.where(lane == 0, 0.0, pltpu.roll(m, 1, 1))
        right = jnp.where(lane == nz - 1, 0.0, pltpu.roll(m, nz - 1, 1))
        low = lower[here, :] if reach is None else lower[here, :] * reach
        beside = (low + upper[here, :]) + (up + down) + (left + right)
        out[here, :] = (
            2.0 * m - before[here, :] + speed[here, :] * (beside - 6.0 * m) + weight * force[here, :]
        )


def sampled_row(planes, info, cell):
    ny, nz = planes[0].shape
    x = cell // (ny * nz) - info[1] * len(planes)
    y = lax.rem(cell // nz, ny)
    z = lax.rem(cell, nz)
    q = jnp.where(info[0] == 1, len(planes) - 1 - x, x)
    lane = lax.broadcasted_iota(jnp.int32, (1, nz), 1)
    row = jnp.zeros((1, nz), jnp.float32)
    for k, plane in enumerate(planes):
        row = jnp.where((lane == z) & (q == k), plane[pl.ds(y, 1), :], row)
    return row


def prep_kernel(info, courant, misfit, states, ce, ci, fe, fi, e0, e1, inner, b0, b1, binner):
    odd = info[0] == 1
    alive = (info[2] == 1).astype(jnp.float32)

    def spread(flip):
        q = (lambda k: 3 - k) if flip else (lambda k: k)
        ce[...], ci[0], ci[1], ci[2] = (courant[q(k)] for k in range(4))
        fe[...], fi[0], fi[1], fi[2] = (misfit[q(k)] for k in range(4))
        for lev, (first, last, mid) in enumerate(((e0, e1, inner), (b0, b1, binner))):
            first[...] = states[lev, q(0)] * alive
            last[...] = states[lev, q(3)] * alive
            mid[0], mid[1] = states[lev, q(1)] * alive, states[lev, q(2)] * alive

    @pl.when(odd)
    def _():
        spread(True)

    @pl.when(jnp.logical_not(odd))
    def _():
        spread(False)


def restrict_kernel(courant, states, rb, rc, tall):
    for xc in range(2):
        rc[xc] = restrict_planes(courant.at[2 * xc], courant.at[2 * xc + 1], tall)
        for lev in range(2):
            rb[lev, xc] = restrict_planes(states.at[lev, 2 * xc], states.at[lev, 2 * xc + 1], tall)


def edge_kernel(level, taken, info, cells, wavelet, e0, e1, inner, b0, off, ce, fe, samples, n0, out_samples):
    reach = info[3].astype(jnp.float32)
    update_plane(e0, off, inner.at[0], b0, ce, fe, wavelet[level], n0, reach)
    out_samples[...] = samples[...]
    if taken is not None:
        planes = (e0, inner.at[0], inner.at[1], e1)
        out_samples[taken : taken + 1, :] = sampled_row(planes, info, cells[taken])


def inner_kernel(level, wavelet, e0, e1, inner, b1, before, on, ci, fi, n1, out):
    weight = wavelet[level]
    update_plane(e1, inner.at[1], on, b1, ci.at[2], fi.at[2], weight, n1)
    update_plane(inner.at[0], e0, inner.at[1], before.at[0], ci.at[0], fi.at[0], weight, out.at[0])
    update_plane(inner.at[1], inner.at[0], e1, before.at[1], ci.at[1], fi.at[1], weight, out.at[1])


def leave_kernel(info, cells, e0, e1, inner, b0, b1, binner, samples, rb, rc, out, sums, tall):
    odd = info[0] == 1
    block = out.shape[2]
    for lev, (first, last, mid) in enumerate(((e0, e1, inner), (b0, b1, binner))):
        sums[0] = restrict_planes(first, mid.at[0], tall)
        sums[1] = restrict_planes(last, mid.at[1], tall)
        for xc in range(2):
            r = jnp.where(odd, sums[1 - xc], sums[xc]) - rb[lev, xc]
            for s in range(SLABS):
                out[s, lev * 2 + xc] = r[PLACE[s] * block : (PLACE[s] + 1) * block, :]
    for xc in range(2):
        for s in range(SLABS):
            out[s, 4 + xc] = rc[xc, PLACE[s] * block : (PLACE[s] + 1) * block, :]
    row = sampled_row((e0, inner.at[0], inner.at[1], e1), info, cells[0])
    count = samples.shape[0]
    at = lax.broadcasted_iota(jnp.int32, (count, 1), 0)
    values = jnp.where(at == 0, jnp.sum(row), jnp.sum(samples[...], axis=1, keepdims=True))
    lane = lax.broadcasted_iota(jnp.int32, (count, 128), 1)
    level = lax.broadcasted_iota(jnp.int32, (count, 128), 0)
    line = jnp.sum(jnp.where(lane == level, values, 0.0), axis=0, keepdims=True)
    for s in range(SLABS):
        out[s, 6] = jnp.broadcast_to(line, (block, 128))


def phi_kernel(has_add, info, flags, state, on, off, speed, son, soff, *rest):
    if has_add:
        add, out, a, b, c = rest
    else:
        out, a, b, c = rest
    odd = info[0] == 1
    live = flags[0].astype(jnp.float32)
    reach = info[4].astype(jnp.float32)
    nx = speed.shape[0] * speed.shape[1]
    block = speed.shape[2]
    tall, nz = 3 * block, 128
    zero = jnp.zeros((tall, nz), jnp.float32)
    a[0], a[nx + 1], b[0], b[nx + 1] = zero, zero, zero, zero

    def fill(above, below, sabove, sbelow, wabove, wbelow):
        for rows, source, ssource, weight in (
            (slice(0, block), above, sabove, wabove),
            (slice(block, 2 * block), state, speed, None),
            (slice(2 * block, tall), below, sbelow, wbelow),
        ):
            scale = live if weight is None else live * weight
            a[1 : nx + 1, rows, :] = source[:, 0:2].reshape(nx, block, nz) * scale
            b[1 : nx + 1, rows, :] = source[:, 2:4].reshape(nx, block, nz) * scale
            line = ssource[...].reshape(nx, block, nz)
            c[:, rows, :] = line if weight is None else line * weight

    @pl.when(odd)
    def _():
        fill(on, off, son, soff, jnp.float32(1.0), reach)

    @pl.when(jnp.logical_not(odd))
    def _():
        fill(off, on, soff, son, reach, jnp.float32(1.0))

    step_x = 4
    lane = lax.broadcasted_iota(jnp.int32, (step_x, tall, nz), 2)

    def turn(now, then):
        def some(k, carry):
            x0 = k * step_x
            m = now[pl.ds(x0 + 1, step_x)]
            beside = now[pl.ds(x0, step_x)] + now[pl.ds(x0 + 2, step_x)]
            beside = beside + pltpu.roll(m, 1, 1) + pltpu.roll(m, tall - 1, 1)
            beside = beside + jnp.where(lane == 0, 0.0, pltpu.roll(m, 1, 2))
            beside = beside + jnp.where(lane == nz - 1, 0.0, pltpu.roll(m, nz - 1, 2))
            then[pl.ds(x0 + 1, step_x)] = (
                2.0 * m - then[pl.ds(x0 + 1, step_x)] + c[pl.ds(x0, step_x)] * (beside - 6.0 * m)
            )
            return carry

        lax.fori_loop(0, nx // step_x, some, 0, unroll=UNROLL)

    def two(_, carry):
        turn(a, b)
        turn(b, a)
        return carry

    lax.fori_loop(0, COARSE // 2, two, 0)
    rows = slice(block, 2 * block)
    one = a[1 : nx + 1, rows, :].reshape(SLABS, 2, block, nz)
    other = b[1 : nx + 1, rows, :].reshape(SLABS, 2, block, nz)
    if has_add:
        one = one + add[:, 0:2]
        other = other + add[:, 2:4]
    out[:, 0:2] = one
    out[:, 2:4] = other


def arrive_kernel(coarse, states, out, tall):
    block = coarse.shape[2]
    nzc = tall.shape[1]
    for lev in range(2):
        for xc in range(2):
            for s in range(SLABS):
                piece = coarse[s, lev * 2 + xc]
                for row in (0, 1):
                    tall[pl.ds(2 * PLACE[s] * block + row, block, stride=2), :] = piece
            fine = dot(tall[...], halving(nzc, 2 * nzc))
            out[lev, 2 * xc] = states[lev, 2 * xc] + fine
            out[lev, 2 * xc + 1] = states[lev, 2 * xc + 1] + fine


def body(courant, misfit, wavelet, source_cells, boundary_states):
    steps = wavelet.shape[0]
    ny, nz = courant.shape[1:]
    nyc, nzc = ny // 2, nz // 2
    block = nyc // SLABS
    slab = lax.axis_index("space")
    tm = lax.axis_index("tm")
    states = boundary_states[0]
    natural = tuple(range(SLABS))
    odd = lax.rem(slab, 2)
    alive = (tm > 0).astype(jnp.int32)
    reach = ((slab > 0) & (slab < SLABS - 1)).astype(jnp.int32)
    creach = ((slab != SNAKE[0]) & (slab != SNAKE[-1])).astype(jnp.int32)
    info = jnp.stack([odd, slab, alive, reach, creach]).astype(jnp.int32)
    ring = [(i, (i + 1) % GROUPS) for i in range(GROUPS)]
    back = [(i, (i - 1) % GROUPS) for i in range(GROUPS)]

    mask = alive.astype(jnp.float32)
    first_off = lax.dynamic_index_in_dim(states[0], 3 * odd, 0, keepdims=False) * mask
    first_on = lax.dynamic_index_in_dim(states[0], 3 - 3 * odd, 0, keepdims=False) * mask
    off = exchange(first_off, natural, 1)
    on = exchange(first_on, natural, 0)
    weights = lax.ppermute(wavelet, "tm", ring)
    cells = lax.ppermute(source_cells, "tm", ring)

    plane = f32(ny, nz)
    ce, ci, fe, fi, e0, e1, inner, b0, b1, binner = call(
        prep_kernel,
        (plane, f32(3, ny, nz)) * 2 + (plane, plane, f32(2, ny, nz)) * 2,
        (info, courant, misfit, states),
        [SM, VM, VM, VM],
    )
    samples = jnp.zeros((steps, nz), jnp.float32)
    for turn in range(steps):
        level = steps - 1 - turn
        n0, samples = call(
            functools.partial(edge_kernel, level, level + 1 if turn else None),
            (plane, f32(steps, nz)),
            (info, cells, weights, e0, e1, inner, b0, off, ce, fe, samples),
            [SM, SM, SM] + [VM] * 8,
        )
        if turn < steps - 1:
            off = exchange(n0, natural, 1)
        if turn == 2:
            gate = lax.optimization_barrier((courant, states, n0))
            rb, rc = call(
                restrict_kernel,
                (f32(2, 2, nyc, nzc), f32(2, nyc, nzc)),
                gate[:2],
                [VM, VM],
                scratch=[pltpu.VMEM((ny, nzc), jnp.float32)],
            )
            rb = lax.ppermute(rb, "tm", ring)
        n1, ninner = call(
            functools.partial(inner_kernel, level),
            (plane, f32(2, ny, nz)),
            (weights, e0, e1, inner, b1, binner, on, ci, fi),
            [SM] + [VM] * 8,
        )
        if turn < steps - 1:
            on = exchange(n1, natural, 0)
        e0, e1, inner, b0, b1, binner = n0, n1, ninner, e0, e1, inner

    pieces = call(
        leave_kernel,
        f32(SLABS, 7, block, nzc),
        (info, cells, e0, e1, inner, b0, b1, binner, samples, rb, rc),
        [SM, SM] + [VM] * 9,
        scratch=[pltpu.VMEM((2, nyc, nzc), jnp.float32), pltpu.VMEM((ny, nzc), jnp.float32)],
    )
    pieces = lax.all_to_all(pieces, "space", 0, 0)
    total = pieces[:, :4]
    speed = pieces[:, 4:6]
    son = exchange(speed, SNAKE, 0)
    soff = exchange(speed, SNAKE, 1)
    line = jnp.sum(pieces[:, 6, 0, :], axis=0)

    def phi(state, add, live):
        sides = (exchange(state, SNAKE, 1), exchange(state, SNAKE, 0))
        nx = SLABS * 2
        args = (info, live, state, sides[1], sides[0], speed, son, soff)
        args = args + (() if add is None else (add,))
        return call(
            functools.partial(phi_kernel, add is not None),
            f32(SLABS, 4, block, nzc),
            args,
            [SM, SM] + [VM] * (len(args) - 2),
            scratch=[pltpu.VMEM((nx + 2, 3 * block, nzc), jnp.float32)] * 2
            + [pltpu.VMEM((nx, 3 * block, nzc), jnp.float32)],
        )

    def later(state, distance, aligned):
        route = []
        for to in range(GROUPS):
            group = to if aligned else (to - 1) % GROUPS
            route.append(((group + distance + 1) % GROUPS, to))
        group = tm if aligned else lax.rem(tm + GROUPS - 1, GROUPS)
        return lax.ppermute(state, "tm", route), (group + distance < GROUPS).astype(jnp.int32)[None]

    moved, live = later(total, 1, False)
    total = phi(moved, total, live)
    moved, live = later(total, 2, False)
    always = jnp.ones((1,), jnp.int32)
    total = phi(phi(moved, None, live), total, always)
    moved, live = later(total, 4, True)
    own = lax.ppermute(total, "tm", back)
    line = lax.ppermute(line, "tm", back)
    own, line = lax.optimization_barrier((own, line))
    for turn in range(4):
        moved = phi(moved, own if turn == 3 else None, always if turn else live)
    gradient = line[:steps]
    coarse = lax.all_to_all(moved, "space", 0, 0)
    updated = call(
        arrive_kernel,
        f32(2, 4, ny, nz),
        (coarse, states),
        [VM, VM],
        scratch=[pltpu.VMEM((ny, nzc), jnp.float32)],
    )
    return (updated[None], gradient)


def solution(mesh):
    placed = (
        P("space", None, None),
        P("space", None, None),
        P("tm"),
        P("tm"),
        P("tm", None, "space", None, None),
    )
    return jax.shard_map(
        body,
        mesh=mesh,
        in_specs=placed,
        out_specs=(P("tm", None, "space", None, None), P("tm")),
        check_vma=False,
    )
```

```python
import functools

import jax
import jax.numpy as jnp
from jax import lax
from jax.experimental import pallas as pl
from jax.experimental.pallas import tpu as pltpu
from jax.sharding import PartitionSpec as P

COARSE = 8
GROUPS = 8
SLABS = 16
ROWS = 32
UNROLL = 8
HIGH = lax.Precision.HIGHEST

SNAKE = tuple(
    y * 4 + z * 2 + c for y in range(4) for z in ((0, 1) if y % 2 == 0 else (1, 0)) for c in (0, 1)
)
PLACE = tuple(SNAKE.index(s) for s in range(SLABS))
VM = pl.BlockSpec(memory_space=pltpu.VMEM)
SM = pl.BlockSpec(memory_space=pltpu.SMEM)
HB = pl.BlockSpec(memory_space=pltpu.HBM)


def exchange(block, order, offset):
    pairs = []
    for row in range(GROUPS):
        base, beside = row * SLABS, (row ^ 1) * SLABS
        for i in range(offset, SLABS - 1, 2):
            here, there = base + order[i], base + order[i + 1]
            pairs += [(here, there), (there, here)]
        if offset:
            pairs += [(base + end, beside + end) for end in (order[0], order[-1])]
    return lax.ppermute(block, ("tm", "space"), pairs)


def call(kernel, out_shapes, args, specs, scratch=(), aliases=None, cost=None):
    return pl.pallas_call(
        kernel,
        out_shape=out_shapes,
        in_specs=specs,
        out_specs=jax.tree.map(lambda _: VM, out_shapes),
        scratch_shapes=list(scratch),
        input_output_aliases=aliases or {},
        cost_estimate=cost,
        compiler_params=pltpu.CompilerParams(vmem_limit_bytes=16 << 20),
    )(*args)


def f32(*shape):
    return jax.ShapeDtypeStruct(shape, jnp.float32)


def halving(rows, cols):
    r = lax.broadcasted_iota(jnp.int32, (rows, cols), 0)
    c = lax.broadcasted_iota(jnp.int32, (rows, cols), 1)
    hit = c // 2 == r if rows < cols else r // 2 == c
    return jnp.where(hit, 1.0, 0.0).astype(jnp.bfloat16)


def dot(a, ones):
    total = None
    for _ in range(3):
        part = a.astype(jnp.bfloat16)
        a = a - part.astype(jnp.float32)
        term = jnp.dot(part, ones, preferred_element_type=jnp.float32)
        total = term if total is None else total + term
    return total


def restrict_planes(first, second, tall):
    ny, nz = first.shape
    tall[...] = dot(first[...] + second[...], halving(nz, nz // 2))
    half = ny // 2
    return (tall[pl.ds(0, half, stride=2), :] + tall[pl.ds(1, half, stride=2), :]) * 0.125


def update_plane(mid, lower, upper, before, speed, force, weight, out, reach=None):
    ny, nz = mid.shape
    lane = lax.broadcasted_iota(jnp.int32, (ROWS, nz), 1)
    row = lax.broadcasted_iota(jnp.int32, (ROWS, nz), 0)
    for r0 in range(0, ny, ROWS):
        here = slice(r0, r0 + ROWS)
        m = mid[here, :]
        if r0 == 0:
            up = jnp.where(row == 0, 0.0, pltpu.roll(m, 1, 0))
        else:
            up = mid[r0 - 1 : r0 - 1 + ROWS, :]
        if r0 + ROWS == ny:
            down = jnp.where(row == ROWS - 1, 0.0, pltpu.roll(m, ROWS - 1, 0))
        else:
            down = mid[r0 + 1 : r0 + 1 + ROWS, :]
        left = jnp.where(lane == 0, 0.0, pltpu.roll(m, 1, 1))
        right = jnp.where(lane == nz - 1, 0.0, pltpu.roll(m, nz - 1, 1))
        low = lower[here, :] if reach is None else lower[here, :] * reach
        beside = (low + upper[here, :]) + (up + down) + (left + right)
        out[here, :] = (
            2.0 * m - before[here, :] + speed[here, :] * (beside - 6.0 * m) + weight * force[here, :]
        )


def sampled_row(planes, info, cell):
    ny, nz = planes[0].shape
    x = cell // (ny * nz) - info[1] * len(planes)
    y = lax.rem(cell // nz, ny)
    z = lax.rem(cell, nz)
    q = jnp.where(info[0] == 1, len(planes) - 1 - x, x)
    lane = lax.broadcasted_iota(jnp.int32, (1, nz), 1)
    row = jnp.zeros((1, nz), jnp.float32)
    for k, plane in enumerate(planes):
        row = jnp.where((lane == z) & (q == k), plane[pl.ds(y, 1), :], row)
    return row


def prep_kernel(info, courant, misfit, states, ce, ci, fe, fi, e0, e1, inner, b0, b1, binner, sems):
    def spread(flip):
        q = (lambda k: 3 - k) if flip else (lambda k: k)
        moves = [(states.at[0, q(0)], e0), (courant.at[q(0)], ce), (misfit.at[q(0)], fe)]
        moves += [(states.at[1, q(0)], b0), (states.at[0, q(3)], e1), (states.at[1, q(3)], b1)]
        for k in range(2):
            moves += [(states.at[0, q(k + 1)], inner.at[k]), (states.at[1, q(k + 1)], binner.at[k])]
        for k in range(3):
            moves += [(courant.at[q(k + 1)], ci.at[k]), (misfit.at[q(k + 1)], fi.at[k])]
        copies = [pltpu.make_async_copy(a, b, sems.at[i]) for i, (a, b) in enumerate(moves)]
        for copy in copies:
            copy.start()
        for copy in copies:
            copy.wait()

    @pl.when(info[0] == 1)
    def _():
        spread(True)

    @pl.when(info[0] == 0)
    def _():
        spread(False)

    @pl.when(info[2] == 0)
    def _():
        for ref in (e0, e1, inner, b0, b1, binner):
            ref[...] = jnp.zeros_like(ref)


def restrict_kernel(courant, states, rb, rc, tall):
    block = rc.shape[2]
    for xc in range(2):
        r = restrict_planes(courant.at[2 * xc], courant.at[2 * xc + 1], tall)
        for s in range(SLABS):
            rc[s, xc] = r[PLACE[s] * block : (PLACE[s] + 1) * block, :]
        for lev in range(2):
            rb[lev, xc] = restrict_planes(states.at[lev, 2 * xc], states.at[lev, 2 * xc + 1], tall)


def edge_kernel(level, weights, reach, e0, inner, b0, off, ce, fe, n0):
    weight = weights[level : level + 1, :]
    update_plane(e0, off, inner.at[0], b0, ce, fe, weight, n0, reach[...])


def inner_kernel(level, taken, info, cells, weights, e0, e1, inner, b1, before, on, ci, fi, samples, n1, out, out_samples):
    weight = weights[level : level + 1, :]
    update_plane(e1, inner.at[1], on, b1, ci.at[2], fi.at[2], weight, n1)
    update_plane(inner.at[0], e0, inner.at[1], before.at[0], ci.at[0], fi.at[0], weight, out.at[0])
    update_plane(inner.at[1], inner.at[0], e1, before.at[1], ci.at[1], fi.at[1], weight, out.at[1])
    out_samples[...] = samples[...]
    if taken is not None:
        planes = (e0, inner.at[0], inner.at[1], e1)
        out_samples[taken : taken + 1, :] = sampled_row(planes, info, cells[taken])


def leave_kernel(info, cells, e0, e1, inner, b0, b1, binner, samples, rb, rc, out, sums, tall):
    odd = info[0] == 1
    block = out.shape[2]
    for lev, (first, last, mid) in enumerate(((e0, e1, inner), (b0, b1, binner))):
        sums[0] = restrict_planes(first, mid.at[0], tall)
        sums[1] = restrict_planes(last, mid.at[1], tall)
        for xc in range(2):
            r = jnp.where(odd, sums[1 - xc], sums[xc]) - rb[lev, xc]
            for s in range(SLABS):
                out[s, lev * 2 + xc] = r[PLACE[s] * block : (PLACE[s] + 1) * block, :]
    for s in range(SLABS):
        out[s, 5:7] = rc[s]
    row = sampled_row((e0, inner.at[0], inner.at[1], e1), info, cells[0])
    count = samples.shape[0]
    at = lax.broadcasted_iota(jnp.int32, (count, 1), 0)
    values = jnp.where(at == 0, jnp.sum(row), jnp.sum(samples[...], axis=1, keepdims=True))
    lane = lax.broadcasted_iota(jnp.int32, (count, 128), 1)
    level = lax.broadcasted_iota(jnp.int32, (count, 128), 0)
    line = jnp.sum(jnp.where(lane == level, values, 0.0), axis=0, keepdims=True)
    for s in range(SLABS):
        out[s, 4] = jnp.broadcast_to(line, (block, 128))


def phi_kernel(has_add, flags, state, on, off, speed, son, soff, *rest):
    if has_add:
        add, out, a, b, c = rest
    else:
        out, a, b, c = rest
    odd = flags[0:1, :] > 0.5
    near = flags[1:2, :]
    nx = speed.shape[0] * speed.shape[1]
    block = speed.shape[2]
    tall, nz = 3 * block, 128
    zero = jnp.zeros((tall, nz), jnp.float32)
    a[0], a[nx + 1], b[0], b[nx + 1] = zero, zero, zero, zero

    def fill(target, mine, other, far):
        far = far.reshape(nx, block, nz) * near
        other = other.reshape(nx, block, nz)
        target(slice(0, block), jnp.where(odd, other, far))
        target(slice(block, 2 * block), mine.reshape(nx, block, nz))
        target(slice(2 * block, tall), jnp.where(odd, far, other))

    def to_a(rows, value):
        a[1 : nx + 1, rows, :] = value

    def to_b(rows, value):
        b[1 : nx + 1, rows, :] = value

    def to_c(rows, value):
        c[:, rows, :] = value

    fill(to_a, state[:, 0:2], on[:, 0:2], off[:, 0:2])
    fill(to_b, state[:, 2:4], on[:, 2:4], off[:, 2:4])
    fill(to_c, speed[...], son[...], soff[...])

    step_x = 4
    lane = lax.broadcasted_iota(jnp.int32, (step_x, tall, nz), 2)

    def turn(now, then):
        def some(k, carry):
            x0 = k * step_x
            m = now[pl.ds(x0 + 1, step_x)]
            beside = now[pl.ds(x0, step_x)] + now[pl.ds(x0 + 2, step_x)]
            beside = beside + pltpu.roll(m, 1, 1) + pltpu.roll(m, tall - 1, 1)
            beside = beside + jnp.where(lane == 0, 0.0, pltpu.roll(m, 1, 2))
            beside = beside + jnp.where(lane == nz - 1, 0.0, pltpu.roll(m, nz - 1, 2))
            then[pl.ds(x0 + 1, step_x)] = (
                2.0 * m - then[pl.ds(x0 + 1, step_x)] + c[pl.ds(x0, step_x)] * (beside - 6.0 * m)
            )
            return carry

        lax.fori_loop(0, nx // step_x, some, 0, unroll=UNROLL)

    def two(_, carry):
        turn(a, b)
        turn(b, a)
        return carry

    lax.fori_loop(0, COARSE // 2, two, 0)
    rows = slice(block, 2 * block)
    one = a[1 : nx + 1, rows, :].reshape(SLABS, 2, block, nz)
    other = b[1 : nx + 1, rows, :].reshape(SLABS, 2, block, nz)
    if has_add:
        one = one + add[:, 0:2]
        other = other + add[:, 2:4]
    out[:, 0:2] = one
    out[:, 2:4] = other


def arrive_kernel(coarse, states, out, tall):
    block = coarse.shape[2]
    nzc = tall.shape[1]
    for lev in range(2):
        for xc in range(2):
            for s in range(SLABS):
                piece = coarse[s, lev * 2 + xc]
                for row in (0, 1):
                    tall[pl.ds(2 * PLACE[s] * block + row, block, stride=2), :] = piece
            fine = dot(tall[...], halving(nzc, 2 * nzc))
            out[lev, 2 * xc] = states[lev, 2 * xc] + fine
            out[lev, 2 * xc + 1] = states[lev, 2 * xc + 1] + fine


def body(courant, misfit, wavelet, source_cells, boundary_states):
    steps = wavelet.shape[0]
    ny, nz = courant.shape[1:]
    nyc, nzc = ny // 2, nz // 2
    block = nyc // SLABS
    slab = lax.axis_index("space")
    tm = lax.axis_index("tm")
    states = boundary_states[0]
    natural = tuple(range(SLABS))
    odd = lax.rem(slab, 2)
    alive = (tm > 0).astype(jnp.int32)
    reach = ((slab > 0) & (slab < SLABS - 1)).astype(jnp.int32)
    creach = ((slab != SNAKE[0]) & (slab != SNAKE[-1])).astype(jnp.int32)
    info = jnp.stack([odd, slab, alive, reach, creach]).astype(jnp.int32)
    ring = [(i, (i + 1) % GROUPS) for i in range(GROUPS)]
    back = [(i, (i - 1) % GROUPS) for i in range(GROUPS)]

    mask = alive.astype(jnp.float32)
    first_off = lax.dynamic_index_in_dim(states[0], 3 * odd, 0, keepdims=False) * mask
    first_on = lax.dynamic_index_in_dim(states[0], 3 - 3 * odd, 0, keepdims=False) * mask
    off = exchange(first_off, natural, 1)
    on = exchange(first_on, natural, 0)
    wave, marks, _ = lax.optimization_barrier((wavelet, source_cells, first_off))
    packed = lax.ppermute(jnp.stack([wave, marks.astype(jnp.float32)]), "tm", ring)
    weights = jnp.broadcast_to(packed[0][:, None], (steps, nz))
    cells = packed[1].astype(jnp.int32)

    plane = f32(ny, nz)
    ce, ci, fe, fi, e0, e1, inner, b0, b1, binner = call(
        prep_kernel,
        (plane, f32(3, ny, nz)) * 2 + (plane, plane, f32(2, ny, nz)) * 2,
        (info, courant, misfit, states),
        [SM, HB, HB, HB],
        scratch=[pltpu.SemaphoreType.DMA((16,))],
    )
    away = jnp.broadcast_to(reach.astype(jnp.float32), (1, nz))
    samples = jnp.zeros((steps, nz), jnp.float32)
    for turn in range(steps):
        level = steps - 1 - turn
        n0 = call(
            functools.partial(edge_kernel, level),
            plane,
            (weights, away, e0, inner, b0, off, ce, fe),
            [VM] * 8,
        )
        if turn < steps - 1:
            off = exchange(n0, natural, 1)
        n1, ninner, samples = call(
            functools.partial(inner_kernel, level, level + 1 if turn else None),
            (plane, f32(2, ny, nz), f32(steps, nz)),
            (info, cells, weights, e0, e1, inner, b1, binner, on, ci, fi, samples),
            [SM, SM] + [VM] * 10,
        )
        if turn == 2:
            gate = lax.optimization_barrier((courant, states, n0))
            rb, speed = call(
                restrict_kernel,
                (f32(2, 2, nyc, nzc), f32(SLABS, 2, block, nzc)),
                gate[:2],
                [VM, VM],
                scratch=[pltpu.VMEM((ny, nzc), jnp.float32)],
            )
            n1, rb, speed = lax.optimization_barrier((n1, rb, speed))
            rb = lax.ppermute(rb, "tm", ring)
        if turn == 8:
            n1, rb = lax.optimization_barrier((n1, rb))
        if turn < steps - 1:
            on = exchange(n1, natural, 0)
        e0, e1, inner, b0, b1, binner = n0, n1, ninner, e0, e1, inner

    pieces = call(
        leave_kernel,
        f32(SLABS, 7, block, nzc),
        (info, cells, e0, e1, inner, b0, b1, binner, samples, rb, speed),
        [SM, SM] + [VM] * 9,
        scratch=[pltpu.VMEM((2, nyc, nzc), jnp.float32), pltpu.VMEM((ny, nzc), jnp.float32)],
    )
    pieces = lax.all_to_all(pieces, "space", 0, 0)
    pieces, speed = pieces[:, :5], pieces[:, 5:7]
    lane = (1, nzc)
    parity = jnp.broadcast_to(odd.astype(jnp.float32), lane)
    near = jnp.broadcast_to(creach.astype(jnp.float32), lane)

    flags = jnp.concatenate([parity, near], axis=0)

    def phi(state, add=None):
        sides = (exchange(state, SNAKE, 1), exchange(state, SNAKE, 0))
        nx = SLABS * 2
        args = (flags, state, sides[1], sides[0], speed, son, soff)
        args = args + (() if add is None else (add,))
        return call(
            functools.partial(phi_kernel, add is not None),
            f32(SLABS, 4, block, nzc),
            args,
            [VM] * len(args),
            scratch=[pltpu.VMEM((nx + 2, 3 * block, nzc), jnp.float32)] * 2
            + [pltpu.VMEM((nx, 3 * block, nzc), jnp.float32)],
        )

    def later(state, distance, aligned):
        route = []
        for to in range(GROUPS):
            group = to if aligned else (to - 1) % GROUPS
            route.append(((group + distance + 1) % GROUPS, to))
        group = tm if aligned else lax.rem(tm + GROUPS - 1, GROUPS)
        return lax.ppermute(state, "tm", route) * (group + distance < GROUPS).astype(jnp.float32)

    soff = exchange(speed, SNAKE, 1)
    son = exchange(speed, SNAKE, 0)
    moved = lax.ppermute(pieces, "tm", back)
    moved, son, soff = lax.optimization_barrier((moved, son, soff))
    gradient = jnp.sum(moved[:, 4, 0, :steps], axis=0)
    moved = moved[:, :4] * (lax.rem(tm + GROUPS - 1, GROUPS) + 1 < GROUPS).astype(jnp.float32)
    total = phi(moved, pieces)
    moved = later(total, 2, False)
    total = phi(phi(moved), total)
    moved = later(total, 4, True)
    own = lax.ppermute(total, "tm", back)
    for turn in range(4):
        moved = phi(moved, own if turn == 3 else None)
        if turn == 1:
            moved, own = lax.optimization_barrier((moved, own))
    coarse = lax.all_to_all(moved, "space", 0, 0)
    updated = call(
        arrive_kernel,
        f32(2, 4, ny, nz),
        (coarse, states),
        [VM, VM],
        scratch=[pltpu.VMEM((ny, nzc), jnp.float32)],
    )
    return (updated[None], gradient)


def solution(mesh):
    placed = (
        P("space", None, None),
        P("space", None, None),
        P("tm"),
        P("tm"),
        P("tm", None, "space", None, None),
    )
    return jax.shard_map(
        body,
        mesh=mesh,
        in_specs=placed,
        out_specs=(P("tm", None, "space", None, None), P("tm")),
        check_vma=False,
    )
```

```python
import functools

import jax
import jax.numpy as jnp
from jax import lax
from jax.experimental import pallas as pl
from jax.experimental.pallas import tpu as pltpu
from jax.sharding import PartitionSpec as P

COARSE = 8
GROUPS = 8
SLABS = 16
ROWS = 32
UNROLL = 8
HIGH = lax.Precision.HIGHEST

SNAKE = tuple(
    y * 4 + z * 2 + c for y in range(4) for z in ((0, 1) if y % 2 == 0 else (1, 0)) for c in (0, 1)
)
PLACE = tuple(SNAKE.index(s) for s in range(SLABS))
VM = pl.BlockSpec(memory_space=pltpu.VMEM)
SM = pl.BlockSpec(memory_space=pltpu.SMEM)
HB = pl.BlockSpec(memory_space=pltpu.HBM)


def exchange(block, order, offset):
    pairs = []
    for row in range(GROUPS):
        base, beside = row * SLABS, (row ^ 1) * SLABS
        for i in range(offset, SLABS - 1, 2):
            here, there = base + order[i], base + order[i + 1]
            pairs += [(here, there), (there, here)]
        if offset:
            pairs += [(base + end, beside + end) for end in (order[0], order[-1])]
    return lax.ppermute(block, ("tm", "space"), pairs)


def call(kernel, out_shapes, args, specs, scratch=(), aliases=None, cost=None):
    return pl.pallas_call(
        kernel,
        out_shape=out_shapes,
        in_specs=specs,
        out_specs=jax.tree.map(lambda _: VM, out_shapes),
        scratch_shapes=list(scratch),
        input_output_aliases=aliases or {},
        cost_estimate=cost,
        compiler_params=pltpu.CompilerParams(vmem_limit_bytes=16 << 20),
    )(*args)


def f32(*shape):
    return jax.ShapeDtypeStruct(shape, jnp.float32)


def halving(rows, cols):
    r = lax.broadcasted_iota(jnp.int32, (rows, cols), 0)
    c = lax.broadcasted_iota(jnp.int32, (rows, cols), 1)
    hit = c // 2 == r if rows < cols else r // 2 == c
    return jnp.where(hit, 1.0, 0.0).astype(jnp.bfloat16)


def dot(a, ones):
    total = None
    for _ in range(3):
        part = a.astype(jnp.bfloat16)
        a = a - part.astype(jnp.float32)
        term = jnp.dot(part, ones, preferred_element_type=jnp.float32)
        total = term if total is None else total + term
    return total


def restrict_planes(first, second, tall):
    ny, nz = first.shape
    tall[...] = dot(first[...] + second[...], halving(nz, nz // 2))
    half = ny // 2
    return (tall[pl.ds(0, half, stride=2), :] + tall[pl.ds(1, half, stride=2), :]) * 0.125


def update_plane(mid, lower, upper, before, speed, force, weight, out, reach=None):
    ny, nz = mid.shape
    lane = lax.broadcasted_iota(jnp.int32, (ROWS, nz), 1)
    row = lax.broadcasted_iota(jnp.int32, (ROWS, nz), 0)
    for r0 in range(0, ny, ROWS):
        here = slice(r0, r0 + ROWS)
        m = mid[here, :]
        if r0 == 0:
            up = jnp.where(row == 0, 0.0, pltpu.roll(m, 1, 0))
        else:
            up = mid[r0 - 1 : r0 - 1 + ROWS, :]
        if r0 + ROWS == ny:
            down = jnp.where(row == ROWS - 1, 0.0, pltpu.roll(m, ROWS - 1, 0))
        else:
            down = mid[r0 + 1 : r0 + 1 + ROWS, :]
        left = jnp.where(lane == 0, 0.0, pltpu.roll(m, 1, 1))
        right = jnp.where(lane == nz - 1, 0.0, pltpu.roll(m, nz - 1, 1))
        low = lower[here, :] if reach is None else lower[here, :] * reach
        if upper is not None:
            low = low + upper[here, :]
        beside = low + (up + down) + (left + right)
        out[here, :] = (
            2.0 * m - before[here, :] + speed[here, :] * (beside - 6.0 * m) + weight * force[here, :]
        )


def sampled_row(planes, info, cell):
    ny, nz = planes[0].shape
    x = cell // (ny * nz) - info[1] * len(planes)
    y = lax.rem(cell // nz, ny)
    z = lax.rem(cell, nz)
    q = jnp.where(info[0] == 1, len(planes) - 1 - x, x)
    lane = lax.broadcasted_iota(jnp.int32, (1, nz), 1)
    row = jnp.zeros((1, nz), jnp.float32)
    for k, plane in enumerate(planes):
        row = jnp.where((lane == z) & (q == k), plane[pl.ds(y, 1), :], row)
    return row


def prep_kernel(info, courant, misfit, states, ce, ci, fe, fi, e0, inner, b0, binner, sems):
    def spread(flip):
        q = (lambda k: 3 - k) if flip else (lambda k: k)
        moves = [(states.at[0, q(0)], e0), (courant.at[q(0)], ce), (misfit.at[q(0)], fe)]
        moves += [(states.at[1, q(0)], b0)]
        for k in range(3):
            moves += [(states.at[0, q(k + 1)], inner.at[k]), (states.at[1, q(k + 1)], binner.at[k])]
            moves += [(courant.at[q(k + 1)], ci.at[k]), (misfit.at[q(k + 1)], fi.at[k])]
        copies = [pltpu.make_async_copy(a, b, sems.at[i]) for i, (a, b) in enumerate(moves)]
        for copy in copies:
            copy.start()
        for copy in copies:
            copy.wait()

    @pl.when(info[0] == 1)
    def _():
        spread(True)

    @pl.when(info[0] == 0)
    def _():
        spread(False)

    @pl.when(info[2] == 0)
    def _():
        for ref in (e0, inner, b0, binner):
            ref[...] = jnp.zeros_like(ref)


def restrict_kernel(courant, states, rb, rc, tall):
    block = rc.shape[2]
    for xc in range(2):
        r = restrict_planes(courant.at[2 * xc], courant.at[2 * xc + 1], tall)
        for s in range(SLABS):
            rc[s, xc] = r[PLACE[s] * block : (PLACE[s] + 1) * block, :]
        for lev in range(2):
            rb[lev, xc] = restrict_planes(states.at[lev, 2 * xc], states.at[lev, 2 * xc + 1], tall)


def edge_kernel(level, weights, reach, e0, inner, b0, off, ce, fe, n0):
    weight = weights[level : level + 1, :]
    update_plane(e0, off, inner.at[0], b0, ce, fe, weight, n0, reach[...])


def inner_kernel(level, taken, info, cells, weights, e0, inner, before, on, ci, fi, samples, n1, out, out_samples, beside):
    weight = weights[level : level + 1, :]
    ny = e0.shape[0]

    def pair(k, carry):
        here = pl.ds(pl.multiple_of(k * ROWS, ROWS), ROWS)
        beside[0, here, :] = e0[here, :] + inner[1, here, :]
        beside[1, here, :] = inner[0, here, :] + inner[2, here, :]
        beside[2, here, :] = inner[1, here, :] + on[here, :]
        return carry

    lax.fori_loop(0, ny // ROWS, pair, 0)

    def plane(k, carry):
        update_plane(inner.at[k], beside.at[k], None, before.at[k], ci.at[k], fi.at[k], weight, out.at[k])
        return carry

    lax.fori_loop(0, 3, plane, 0)

    def copy(k, carry):
        here = pl.ds(pl.multiple_of(k * ROWS, ROWS), ROWS)
        n1[here, :] = out[2, here, :]
        return carry

    lax.fori_loop(0, ny // ROWS, copy, 0)
    out_samples[...] = samples[...]
    if taken is not None:
        planes = (e0, inner.at[0], inner.at[1], inner.at[2])
        out_samples[taken : taken + 1, :] = sampled_row(planes, info, cells[taken])


def leave_kernel(info, cells, e0, inner, b0, binner, samples, rb, rc, out, sums, tall):
    odd = info[0] == 1
    block = out.shape[2]
    for lev, (first, mid) in enumerate(((e0, inner), (b0, binner))):
        sums[0] = restrict_planes(first, mid.at[0], tall)
        sums[1] = restrict_planes(mid.at[1], mid.at[2], tall)
        for xc in range(2):
            r = jnp.where(odd, sums[1 - xc], sums[xc]) - rb[lev, xc]
            for s in range(SLABS):
                out[s, lev * 2 + xc] = r[PLACE[s] * block : (PLACE[s] + 1) * block, :]
    for s in range(SLABS):
        out[s, 5:7] = rc[s]
    row = sampled_row((e0, inner.at[0], inner.at[1], inner.at[2]), info, cells[0])
    count = samples.shape[0]
    at = lax.broadcasted_iota(jnp.int32, (count, 1), 0)
    values = jnp.where(at == 0, jnp.sum(row), jnp.sum(samples[...], axis=1, keepdims=True))
    lane = lax.broadcasted_iota(jnp.int32, (count, 128), 1)
    level = lax.broadcasted_iota(jnp.int32, (count, 128), 0)
    line = jnp.sum(jnp.where(lane == level, values, 0.0), axis=0, keepdims=True)
    for s in range(SLABS):
        out[s, 4] = jnp.broadcast_to(line, (block, 128))


def phi_kernel(has_add, flags, state, on, off, speed, son, soff, *rest):
    if has_add:
        add, out, a, b, c = rest
    else:
        out, a, b, c = rest
    odd = flags[0:1, :] > 0.5
    near = flags[1:2, :]
    nx = speed.shape[0] * speed.shape[1]
    block = speed.shape[2]
    tall, nz = 3 * block, 128
    zero = jnp.zeros((tall, nz), jnp.float32)
    a[0], a[nx + 1], b[0], b[nx + 1] = zero, zero, zero, zero

    def fill(target, mine, other, far):
        far = far.reshape(nx, block, nz) * near
        other = other.reshape(nx, block, nz)
        target(slice(0, block), jnp.where(odd, other, far))
        target(slice(block, 2 * block), mine.reshape(nx, block, nz))
        target(slice(2 * block, tall), jnp.where(odd, far, other))

    def to_a(rows, value):
        a[1 : nx + 1, rows, :] = value

    def to_b(rows, value):
        b[1 : nx + 1, rows, :] = value

    def to_c(rows, value):
        c[:, rows, :] = value

    fill(to_a, state[:, 0:2], on[:, 0:2], off[:, 0:2])
    fill(to_b, state[:, 2:4], on[:, 2:4], off[:, 2:4])
    fill(to_c, speed[...], son[...], soff[...])

    step_x = 4
    lane = lax.broadcasted_iota(jnp.int32, (step_x, tall, nz), 2)

    def turn(now, then):
        def some(k, carry):
            x0 = k * step_x
            m = now[pl.ds(x0 + 1, step_x)]
            beside = now[pl.ds(x0, step_x)] + now[pl.ds(x0 + 2, step_x)]
            beside = beside + pltpu.roll(m, 1, 1) + pltpu.roll(m, tall - 1, 1)
            beside = beside + jnp.where(lane == 0, 0.0, pltpu.roll(m, 1, 2))
            beside = beside + jnp.where(lane == nz - 1, 0.0, pltpu.roll(m, nz - 1, 2))
            then[pl.ds(x0 + 1, step_x)] = (
                2.0 * m - then[pl.ds(x0 + 1, step_x)] + c[pl.ds(x0, step_x)] * (beside - 6.0 * m)
            )
            return carry

        lax.fori_loop(0, nx // step_x, some, 0, unroll=UNROLL)

    def two(_, carry):
        turn(a, b)
        turn(b, a)
        return carry

    lax.fori_loop(0, COARSE // 2, two, 0)
    rows = slice(block, 2 * block)
    one = a[1 : nx + 1, rows, :].reshape(SLABS, 2, block, nz)
    other = b[1 : nx + 1, rows, :].reshape(SLABS, 2, block, nz)
    if has_add:
        one = one + add[:, 0:2]
        other = other + add[:, 2:4]
    out[:, 0:2] = one
    out[:, 2:4] = other


def arrive_kernel(coarse, states, out, tall):
    block = coarse.shape[2]
    nzc = tall.shape[1]
    for lev in range(2):
        for xc in range(2):
            for s in range(SLABS):
                piece = coarse[s, lev * 2 + xc]
                for row in (0, 1):
                    tall[pl.ds(2 * PLACE[s] * block + row, block, stride=2), :] = piece
            fine = dot(tall[...], halving(nzc, 2 * nzc))
            out[lev, 2 * xc] = states[lev, 2 * xc] + fine
            out[lev, 2 * xc + 1] = states[lev, 2 * xc + 1] + fine


def body(courant, misfit, wavelet, source_cells, boundary_states):
    steps = wavelet.shape[0]
    ny, nz = courant.shape[1:]
    nyc, nzc = ny // 2, nz // 2
    block = nyc // SLABS
    slab = lax.axis_index("space")
    tm = lax.axis_index("tm")
    states = boundary_states[0]
    natural = tuple(range(SLABS))
    odd = lax.rem(slab, 2)
    alive = (tm > 0).astype(jnp.int32)
    reach = ((slab > 0) & (slab < SLABS - 1)).astype(jnp.int32)
    creach = ((slab != SNAKE[0]) & (slab != SNAKE[-1])).astype(jnp.int32)
    info = jnp.stack([odd, slab, alive, reach, creach]).astype(jnp.int32)
    ring = [(i, (i + 1) % GROUPS) for i in range(GROUPS)]
    back = [(i, (i - 1) % GROUPS) for i in range(GROUPS)]

    mask = alive.astype(jnp.float32)
    first_off = lax.dynamic_index_in_dim(states[0], 3 * odd, 0, keepdims=False) * mask
    first_on = lax.dynamic_index_in_dim(states[0], 3 - 3 * odd, 0, keepdims=False) * mask
    off = exchange(first_off, natural, 1)
    on = exchange(first_on, natural, 0)
    wave, marks, _ = lax.optimization_barrier((wavelet, source_cells, first_off))
    packed = lax.ppermute(jnp.stack([wave, marks.astype(jnp.float32)]), "tm", ring)
    weights = jnp.broadcast_to(packed[0][:, None], (steps, nz))
    cells = packed[1].astype(jnp.int32)

    plane = f32(ny, nz)
    ce, ci, fe, fi, e0, inner, b0, binner = call(
        prep_kernel,
        (plane, f32(3, ny, nz)) * 4,
        (info, courant, misfit, states),
        [SM, HB, HB, HB],
        scratch=[pltpu.SemaphoreType.DMA((16,))],
    )
    away = jnp.broadcast_to(reach.astype(jnp.float32), (1, nz))
    samples = jnp.zeros((steps, nz), jnp.float32)
    for turn in range(steps):
        level = steps - 1 - turn
        n0 = call(
            functools.partial(edge_kernel, level),
            plane,
            (weights, away, e0, inner, b0, off, ce, fe),
            [VM] * 8,
        )
        if turn < steps - 1:
            off = exchange(n0, natural, 1)
        n1, ninner, samples = call(
            functools.partial(inner_kernel, level, level + 1 if turn else None),
            (plane, f32(3, ny, nz), f32(steps, nz)),
            (info, cells, weights, e0, inner, binner, on, ci, fi, samples),
            [SM, SM] + [VM] * 8,
            scratch=[pltpu.VMEM((3, ny, nz), jnp.float32)],
        )
        if turn == 2:
            gate = lax.optimization_barrier((courant, states, n0))
            rb, speed = call(
                restrict_kernel,
                (f32(2, 2, nyc, nzc), f32(SLABS, 2, block, nzc)),
                gate[:2],
                [VM, VM],
                scratch=[pltpu.VMEM((ny, nzc), jnp.float32)],
            )
            n1, rb, speed = lax.optimization_barrier((n1, rb, speed))
            rb = lax.ppermute(rb, "tm", ring)
        if turn == 8:
            n1, rb = lax.optimization_barrier((n1, rb))
        if turn < steps - 1:
            on = exchange(n1, natural, 0)
        e0, inner, b0, binner = n0, ninner, e0, inner

    pieces = call(
        leave_kernel,
        f32(SLABS, 7, block, nzc),
        (info, cells, e0, inner, b0, binner, samples, rb, speed),
        [SM, SM] + [VM] * 7,
        scratch=[pltpu.VMEM((2, nyc, nzc), jnp.float32), pltpu.VMEM((ny, nzc), jnp.float32)],
    )
    pieces = lax.all_to_all(pieces, "space", 0, 0)
    pieces, speed = pieces[:, :5], pieces[:, 5:7]
    lane = (1, nzc)
    parity = jnp.broadcast_to(odd.astype(jnp.float32), lane)
    near = jnp.broadcast_to(creach.astype(jnp.float32), lane)

    flags = jnp.concatenate([parity, near], axis=0)

    def phi(state, add=None):
        sides = (exchange(state, SNAKE, 1), exchange(state, SNAKE, 0))
        nx = SLABS * 2
        args = (flags, state, sides[1], sides[0], speed, son, soff)
        args = args + (() if add is None else (add,))
        return call(
            functools.partial(phi_kernel, add is not None),
            f32(SLABS, 4, block, nzc),
            args,
            [VM] * len(args),
            scratch=[pltpu.VMEM((nx + 2, 3 * block, nzc), jnp.float32)] * 2
            + [pltpu.VMEM((nx, 3 * block, nzc), jnp.float32)],
        )

    def later(state, distance, aligned):
        route = []
        for to in range(GROUPS):
            group = to if aligned else (to - 1) % GROUPS
            route.append(((group + distance + 1) % GROUPS, to))
        group = tm if aligned else lax.rem(tm + GROUPS - 1, GROUPS)
        return lax.ppermute(state, "tm", route) * (group + distance < GROUPS).astype(jnp.float32)

    soff = exchange(speed, SNAKE, 1)
    son = exchange(speed, SNAKE, 0)
    moved = lax.ppermute(pieces, "tm", back)
    moved, son, soff = lax.optimization_barrier((moved, son, soff))
    gradient = jnp.sum(moved[:, 4, 0, :steps], axis=0)
    moved = moved[:, :4] * (lax.rem(tm + GROUPS - 1, GROUPS) + 1 < GROUPS).astype(jnp.float32)
    total = phi(moved, pieces)
    moved = later(total, 2, False)
    total = phi(phi(moved), total)
    moved = later(total, 4, True)
    own = lax.ppermute(total, "tm", back)
    for turn in range(4):
        moved = phi(moved, own if turn == 3 else None)
        if turn == 1:
            moved, own = lax.optimization_barrier((moved, own))
    coarse = lax.all_to_all(moved, "space", 0, 0)
    updated = call(
        arrive_kernel,
        f32(2, 4, ny, nz),
        (coarse, states),
        [VM, VM],
        scratch=[pltpu.VMEM((ny, nzc), jnp.float32)],
    )
    return (updated[None], gradient)


def solution(mesh):
    placed = (
        P("space", None, None),
        P("space", None, None),
        P("tm"),
        P("tm"),
        P("tm", None, "space", None, None),
    )
    return jax.shard_map(
        body,
        mesh=mesh,
        in_specs=placed,
        out_specs=(P("tm", None, "space", None, None), P("tm")),
        check_vma=False,
    )
```

```python
import functools

import jax
import jax.numpy as jnp
from jax import lax
from jax.experimental import pallas as pl
from jax.experimental.pallas import tpu as pltpu
from jax.sharding import PartitionSpec as P

COARSE = 8
GROUPS = 8
SLABS = 16
ROWS = 32
UNROLL = 8
HIGH = lax.Precision.HIGHEST

TOUR = tuple(y * 4 + c for y in range(4) for c in (0, 1)) + tuple(
    y * 4 + 2 + c for y in reversed(range(4)) for c in (0, 1)
)
TOUR = TOUR[1:] + TOUR[:1]
PLACE = tuple(TOUR.index(s) for s in range(SLABS))
VM = pl.BlockSpec(memory_space=pltpu.VMEM)
SM = pl.BlockSpec(memory_space=pltpu.SMEM)
HB = pl.BlockSpec(memory_space=pltpu.HBM)


def trade(block, pairs, ends=()):
    route = []
    for row in range(GROUPS):
        base, beside = row * SLABS, (row ^ 1) * SLABS
        for here, there in pairs:
            route += [(base + here, base + there), (base + there, base + here)]
        route += [(base + end, beside + end) for end in ends]
    return lax.ppermute(block, ("tm", "space"), route)


def away_side(block):
    return trade(block, [(TOUR[i], TOUR[i + 1]) for i in range(0, SLABS, 2)])


def chip_side(block):
    return trade(block, [(TOUR[i], TOUR[(i + 1) % SLABS]) for i in range(1, SLABS, 2)])


def off_chip(plane):
    return trade(plane, [(i, i + 1) for i in range(1, SLABS - 1, 2)], (0, SLABS - 1))


def on_chip(plane):
    return trade(plane, [(i, i + 1) for i in range(0, SLABS, 2)])


def call(kernel, out_shapes, args, specs, scratch=(), aliases=None, cost=None):
    return pl.pallas_call(
        kernel,
        out_shape=out_shapes,
        in_specs=specs,
        out_specs=jax.tree.map(lambda _: VM, out_shapes),
        scratch_shapes=list(scratch),
        input_output_aliases=aliases or {},
        cost_estimate=cost,
        compiler_params=pltpu.CompilerParams(vmem_limit_bytes=16 << 20),
    )(*args)


def f32(*shape):
    return jax.ShapeDtypeStruct(shape, jnp.float32)


def halving(rows, cols):
    r = lax.broadcasted_iota(jnp.int32, (rows, cols), 0)
    c = lax.broadcasted_iota(jnp.int32, (rows, cols), 1)
    hit = c // 2 == r if rows < cols else r // 2 == c
    return jnp.where(hit, 1.0, 0.0).astype(jnp.bfloat16)


def dot(a, ones):
    total = None
    for _ in range(3):
        part = a.astype(jnp.bfloat16)
        a = a - part.astype(jnp.float32)
        term = jnp.dot(part, ones, preferred_element_type=jnp.float32)
        total = term if total is None else total + term
    return total


def restrict_planes(first, second, tall):
    ny, nz = first.shape
    tall[...] = dot(first[...] + second[...], halving(nz, nz // 2))
    half = ny // 2
    return (tall[pl.ds(0, half, stride=2), :] + tall[pl.ds(1, half, stride=2), :]) * 0.125


def update_plane(mid, lower, upper, before, speed, force, weight, out, reach=None):
    ny, nz = mid.shape
    lane = lax.broadcasted_iota(jnp.int32, (ROWS, nz), 1)
    row = lax.broadcasted_iota(jnp.int32, (ROWS, nz), 0)
    for r0 in range(0, ny, ROWS):
        here = slice(r0, r0 + ROWS)
        m = mid[here, :]
        if r0 == 0:
            up = jnp.where(row == 0, 0.0, pltpu.roll(m, 1, 0))
        else:
            up = mid[r0 - 1 : r0 - 1 + ROWS, :]
        if r0 + ROWS == ny:
            down = jnp.where(row == ROWS - 1, 0.0, pltpu.roll(m, ROWS - 1, 0))
        else:
            down = mid[r0 + 1 : r0 + 1 + ROWS, :]
        left = jnp.where(lane == 0, 0.0, pltpu.roll(m, 1, 1))
        right = jnp.where(lane == nz - 1, 0.0, pltpu.roll(m, nz - 1, 1))
        low = lower[here, :] if reach is None else lower[here, :] * reach
        if upper is not None:
            low = low + upper[here, :]
        beside = low + (up + down) + (left + right)
        out[here, :] = (
            2.0 * m - before[here, :] + speed[here, :] * (beside - 6.0 * m) + weight * force[here, :]
        )


def sampled_row(planes, info, cell):
    ny, nz = planes[0].shape
    x = cell // (ny * nz) - info[1] * len(planes)
    y = lax.rem(cell // nz, ny)
    z = lax.rem(cell, nz)
    q = jnp.where(info[0] == 1, len(planes) - 1 - x, x)
    lane = lax.broadcasted_iota(jnp.int32, (1, nz), 1)
    row = jnp.zeros((1, nz), jnp.float32)
    for k, plane in enumerate(planes):
        row = jnp.where((lane == z) & (q == k), plane[pl.ds(y, 1), :], row)
    return row


def first_kernel(info, states, off, on, sems):
    def fetch(near, far):
        copies = [
            pltpu.make_async_copy(states.at[0, near], off, sems.at[0]),
            pltpu.make_async_copy(states.at[0, far], on, sems.at[1]),
        ]
        for copy in copies:
            copy.start()
        for copy in copies:
            copy.wait()

    @pl.when(info[0] == 1)
    def _():
        fetch(3, 0)

    @pl.when(info[0] == 0)
    def _():
        fetch(0, 3)

    @pl.when(info[2] == 0)
    def _():
        off[...] = jnp.zeros_like(off)
        on[...] = jnp.zeros_like(on)


def prep_kernel(info, courant, misfit, states, ce, ci, fe, fi, e0, inner, b0, binner, sems):
    def spread(flip):
        q = (lambda k: 3 - k) if flip else (lambda k: k)
        moves = [(states.at[0, q(0)], e0), (courant.at[q(0)], ce), (misfit.at[q(0)], fe)]
        moves += [(states.at[1, q(0)], b0)]
        for k in range(3):
            moves += [(states.at[0, q(k + 1)], inner.at[k]), (states.at[1, q(k + 1)], binner.at[k])]
            moves += [(courant.at[q(k + 1)], ci.at[k]), (misfit.at[q(k + 1)], fi.at[k])]
        copies = [pltpu.make_async_copy(a, b, sems.at[i]) for i, (a, b) in enumerate(moves)]
        for copy in copies:
            copy.start()
        for copy in copies:
            copy.wait()

    @pl.when(info[0] == 1)
    def _():
        spread(True)

    @pl.when(info[0] == 0)
    def _():
        spread(False)

    @pl.when(info[2] == 0)
    def _():
        for ref in (e0, inner, b0, binner):
            ref[...] = jnp.zeros_like(ref)


def restrict_kernel(courant, states, rb, rc, tall):
    block = rc.shape[2]
    for xc in range(2):
        r = restrict_planes(courant.at[2 * xc], courant.at[2 * xc + 1], tall)
        for s in range(SLABS):
            rc[s, xc] = r[PLACE[s] * block : (PLACE[s] + 1) * block, :]
        for lev in range(2):
            rb[lev, xc] = restrict_planes(states.at[lev, 2 * xc], states.at[lev, 2 * xc + 1], tall)


def edge_kernel(level, weights, reach, e0, inner, b0, off, ce, fe, n0):
    weight = weights[level : level + 1, :]
    update_plane(e0, off, inner.at[0], b0, ce, fe, weight, n0, reach[...])


def inner_kernel(level, taken, info, cells, weights, e0, inner, before, on, ci, fi, samples, n1, out, out_samples, beside):
    weight = weights[level : level + 1, :]
    ny = e0.shape[0]

    def pair(k, carry):
        here = pl.ds(pl.multiple_of(k * ROWS, ROWS), ROWS)
        beside[0, here, :] = e0[here, :] + inner[1, here, :]
        beside[1, here, :] = inner[0, here, :] + inner[2, here, :]
        beside[2, here, :] = inner[1, here, :] + on[here, :]
        return carry

    lax.fori_loop(0, ny // ROWS, pair, 0)

    def plane(k, carry):
        update_plane(inner.at[k], beside.at[k], None, before.at[k], ci.at[k], fi.at[k], weight, out.at[k])
        return carry

    lax.fori_loop(0, 3, plane, 0)

    def copy(k, carry):
        here = pl.ds(pl.multiple_of(k * ROWS, ROWS), ROWS)
        n1[here, :] = out[2, here, :]
        return carry

    lax.fori_loop(0, ny // ROWS, copy, 0)
    out_samples[...] = samples[...]
    if taken is not None:
        planes = (e0, inner.at[0], inner.at[1], inner.at[2])
        out_samples[taken : taken + 1, :] = sampled_row(planes, info, cells[taken])


def leave_kernel(info, cells, e0, inner, b0, binner, samples, rb, rc, out, sums, tall):
    odd = info[0] == 1
    block = out.shape[2]
    for lev, (first, mid) in enumerate(((e0, inner), (b0, binner))):
        sums[0] = restrict_planes(first, mid.at[0], tall)
        sums[1] = restrict_planes(mid.at[1], mid.at[2], tall)
        for xc in range(2):
            r = jnp.where(odd, sums[1 - xc], sums[xc]) - rb[lev, xc]
            for s in range(SLABS):
                out[s, lev * 2 + xc] = r[PLACE[s] * block : (PLACE[s] + 1) * block, :]
    for s in range(SLABS):
        out[s, 5:7] = rc[s]
    row = sampled_row((e0, inner.at[0], inner.at[1], inner.at[2]), info, cells[0])
    count = samples.shape[0]
    at = lax.broadcasted_iota(jnp.int32, (count, 1), 0)
    values = jnp.where(at == 0, jnp.sum(row), jnp.sum(samples[...], axis=1, keepdims=True))
    lane = lax.broadcasted_iota(jnp.int32, (count, 128), 1)
    level = lax.broadcasted_iota(jnp.int32, (count, 128), 0)
    line = jnp.sum(jnp.where(lane == level, values, 0.0), axis=0, keepdims=True)
    for s in range(SLABS):
        out[s, 4] = jnp.broadcast_to(line, (block, 128))


def phi_kernel(has_add, flags, state, on, off, speed, son, soff, *rest):
    if has_add:
        add, out, a, b, c = rest
    else:
        out, a, b, c = rest
    odd = flags[0:1, :] > 0.5
    near = flags[1:2, :]
    nx = speed.shape[0] * speed.shape[1]
    block = speed.shape[2]
    tall, nz = 3 * block, 128
    zero = jnp.zeros((tall, nz), jnp.float32)
    a[0], a[nx + 1], b[0], b[nx + 1] = zero, zero, zero, zero

    def fill(target, mine, other, far):
        far = far.reshape(nx, block, nz)
        other = other.reshape(nx, block, nz) * near
        target(slice(0, block), jnp.where(odd, other, far))
        target(slice(block, 2 * block), mine.reshape(nx, block, nz))
        target(slice(2 * block, tall), jnp.where(odd, far, other))

    def to_a(rows, value):
        a[1 : nx + 1, rows, :] = value

    def to_b(rows, value):
        b[1 : nx + 1, rows, :] = value

    def to_c(rows, value):
        c[:, rows, :] = value

    fill(to_a, state[:, 0:2], on[:, 0:2], off[:, 0:2])
    fill(to_b, state[:, 2:4], on[:, 2:4], off[:, 2:4])
    fill(to_c, speed[...], son[...], soff[...])

    step_x = 4
    lane = lax.broadcasted_iota(jnp.int32, (step_x, tall, nz), 2)

    def turn(now, then):
        def some(k, carry):
            x0 = k * step_x
            m = now[pl.ds(x0 + 1, step_x)]
            beside = now[pl.ds(x0, step_x)] + now[pl.ds(x0 + 2, step_x)]
            beside = beside + pltpu.roll(m, 1, 1) + pltpu.roll(m, tall - 1, 1)
            beside = beside + jnp.where(lane == 0, 0.0, pltpu.roll(m, 1, 2))
            beside = beside + jnp.where(lane == nz - 1, 0.0, pltpu.roll(m, nz - 1, 2))
            then[pl.ds(x0 + 1, step_x)] = (
                2.0 * m - then[pl.ds(x0 + 1, step_x)] + c[pl.ds(x0, step_x)] * (beside - 6.0 * m)
            )
            return carry

        lax.fori_loop(0, nx // step_x, some, 0, unroll=UNROLL)

    def two(_, carry):
        turn(a, b)
        turn(b, a)
        return carry

    lax.fori_loop(0, COARSE // 2, two, 0)
    rows = slice(block, 2 * block)
    one = a[1 : nx + 1, rows, :].reshape(SLABS, 2, block, nz)
    other = b[1 : nx + 1, rows, :].reshape(SLABS, 2, block, nz)
    if has_add:
        one = one + add[:, 0:2]
        other = other + add[:, 2:4]
    out[:, 0:2] = one
    out[:, 2:4] = other


def arrive_kernel(coarse, states, out, tall):
    block = coarse.shape[2]
    nzc = tall.shape[1]
    for lev in range(2):
        for xc in range(2):
            for s in range(SLABS):
                piece = coarse[s, lev * 2 + xc]
                for row in (0, 1):
                    tall[pl.ds(2 * PLACE[s] * block + row, block, stride=2), :] = piece
            fine = dot(tall[...], halving(nzc, 2 * nzc))
            out[lev, 2 * xc] = states[lev, 2 * xc] + fine
            out[lev, 2 * xc + 1] = states[lev, 2 * xc + 1] + fine


def body(courant, misfit, wavelet, source_cells, boundary_states):
    steps = wavelet.shape[0]
    ny, nz = courant.shape[1:]
    nyc, nzc = ny // 2, nz // 2
    block = nyc // SLABS
    slab = lax.axis_index("space")
    tm = lax.axis_index("tm")
    states = boundary_states[0]
    odd = lax.rem(slab, 2)
    alive = (tm > 0).astype(jnp.int32)
    reach = ((slab > 0) & (slab < SLABS - 1)).astype(jnp.int32)
    creach = ((slab != TOUR[0]) & (slab != TOUR[-1])).astype(jnp.int32)
    info = jnp.stack([odd, slab, alive, reach, creach]).astype(jnp.int32)
    ring = [(i, (i + 1) % GROUPS) for i in range(GROUPS)]
    back = [(i, (i - 1) % GROUPS) for i in range(GROUPS)]

    plane = f32(ny, nz)
    in_hbm = [pltpu.with_memory_space_constraint(x, pltpu.HBM) for x in (courant, misfit, states)]
    first_off, first_on = call(
        first_kernel,
        (plane, plane),
        (info, in_hbm[2]),
        [SM, HB],
        scratch=[pltpu.SemaphoreType.DMA((2,))],
    )
    off = off_chip(first_off)
    on = on_chip(first_on)
    wave, marks, _ = lax.optimization_barrier((wavelet, source_cells, first_off))
    packed = lax.ppermute(jnp.stack([wave, marks.astype(jnp.float32)]), "tm", ring)
    weights = jnp.broadcast_to(packed[0][:, None], (steps, nz))
    cells = packed[1].astype(jnp.int32)

    ce, ci, fe, fi, e0, inner, b0, binner = call(
        prep_kernel,
        (plane, f32(3, ny, nz)) * 4,
        (info, *in_hbm),
        [SM, HB, HB, HB],
        scratch=[pltpu.SemaphoreType.DMA((16,))],
    )
    away = jnp.broadcast_to(reach.astype(jnp.float32), (1, nz))
    samples = jnp.zeros((steps, nz), jnp.float32)
    for turn in range(steps):
        level = steps - 1 - turn
        n0 = call(
            functools.partial(edge_kernel, level),
            plane,
            (weights, away, e0, inner, b0, off, ce, fe),
            [VM] * 8,
        )
        if turn < steps - 1:
            off = off_chip(n0)
        n1, ninner, samples = call(
            functools.partial(inner_kernel, level, level + 1 if turn else None),
            (plane, f32(3, ny, nz), f32(steps, nz)),
            (info, cells, weights, e0, inner, binner, on, ci, fi, samples),
            [SM, SM] + [VM] * 8,
            scratch=[pltpu.VMEM((3, ny, nz), jnp.float32)],
        )
        if turn == 2:
            gate = lax.optimization_barrier((courant, states, n0))
            rb, speed = call(
                restrict_kernel,
                (f32(2, 2, nyc, nzc), f32(SLABS, 2, block, nzc)),
                gate[:2],
                [VM, VM],
                scratch=[pltpu.VMEM((ny, nzc), jnp.float32)],
            )
            n1, rb, speed = lax.optimization_barrier((n1, rb, speed))
            rb = lax.ppermute(rb, "tm", ring)
        if turn == 8:
            n1, rb = lax.optimization_barrier((n1, rb))
        if turn < steps - 1:
            on = on_chip(n1)
        e0, inner, b0, binner = n0, ninner, e0, inner

    pieces = call(
        leave_kernel,
        f32(SLABS, 7, block, nzc),
        (info, cells, e0, inner, b0, binner, samples, rb, speed),
        [SM, SM] + [VM] * 7,
        scratch=[pltpu.VMEM((2, nyc, nzc), jnp.float32), pltpu.VMEM((ny, nzc), jnp.float32)],
    )
    pieces = lax.all_to_all(pieces, "space", 0, 0)
    pieces, speed = pieces[:, :5], pieces[:, 5:7]
    lane = (1, nzc)
    parity = jnp.broadcast_to(odd.astype(jnp.float32), lane)
    near = jnp.broadcast_to(creach.astype(jnp.float32), lane)

    flags = jnp.concatenate([parity, near], axis=0)

    def phi(state, add=None):
        sides = (away_side(state), chip_side(state))
        nx = SLABS * 2
        args = (flags, state, sides[1], sides[0], speed, son, soff)
        args = args + (() if add is None else (add,))
        return call(
            functools.partial(phi_kernel, add is not None),
            f32(SLABS, 4, block, nzc),
            args,
            [VM] * len(args),
            scratch=[pltpu.VMEM((nx + 2, 3 * block, nzc), jnp.float32)] * 2
            + [pltpu.VMEM((nx, 3 * block, nzc), jnp.float32)],
        )

    def later(state, distance, aligned):
        route = []
        for to in range(GROUPS):
            group = to if aligned else (to - 1) % GROUPS
            route.append(((group + distance + 1) % GROUPS, to))
        group = tm if aligned else lax.rem(tm + GROUPS - 1, GROUPS)
        return lax.ppermute(state, "tm", route) * (group + distance < GROUPS).astype(jnp.float32)

    soff = away_side(speed)
    son = chip_side(speed)
    moved = lax.ppermute(pieces, "tm", back)
    moved, son, soff = lax.optimization_barrier((moved, son, soff))
    gradient = jnp.sum(moved[:, 4, 0, :], axis=0)[:steps]
    moved, gradient = lax.optimization_barrier((moved, gradient))
    moved = moved[:, :4] * (lax.rem(tm + GROUPS - 1, GROUPS) + 1 < GROUPS).astype(jnp.float32)
    total = phi(moved, pieces)
    moved = later(total, 2, False)
    total = phi(phi(moved), total)
    moved = later(total, 4, True)
    own = lax.ppermute(total, "tm", back)
    for turn in range(4):
        moved = phi(moved, own if turn == 3 else None)
        if turn == 1:
            moved, own = lax.optimization_barrier((moved, own))
    coarse = lax.all_to_all(moved, "space", 0, 0)
    updated = call(
        arrive_kernel,
        f32(2, 4, ny, nz),
        (coarse, states),
        [VM, VM],
        scratch=[pltpu.VMEM((ny, nzc), jnp.float32)],
    )
    return (updated[None], gradient)


def solution(mesh):
    placed = (
        P("space", None, None),
        P("space", None, None),
        P("tm"),
        P("tm"),
        P("tm", None, "space", None, None),
    )
    return jax.shard_map(
        body,
        mesh=mesh,
        in_specs=placed,
        out_specs=(P("tm", None, "space", None, None), P("tm")),
        check_vma=False,
    )
```

```python
import functools

import jax
import jax.numpy as jnp
from jax import lax
from jax.experimental import pallas as pl
from jax.experimental.pallas import tpu as pltpu
from jax.sharding import PartitionSpec as P


COARSE = 8
GROUPS = 8
SLABS = 16
ROWS = 32
UNROLL = 8

TOUR = tuple(y * 4 + c for y in range(4) for c in (0, 1)) + tuple(
    y * 4 + 2 + c for y in reversed(range(4)) for c in (0, 1)
)
TOUR = TOUR[1:] + TOUR[:1]
PLACE = tuple(TOUR.index(s) for s in range(SLABS))
VM = pl.BlockSpec(memory_space=pltpu.VMEM)
SM = pl.BlockSpec(memory_space=pltpu.SMEM)
HB = pl.BlockSpec(memory_space=pltpu.HBM)


def trade(block, pairs, ends=()):
    route = []
    for row in range(GROUPS):
        base, beside = row * SLABS, (row ^ 1) * SLABS
        for here, there in pairs:
            route += [(base + here, base + there), (base + there, base + here)]
        route += [(base + end, beside + end) for end in ends]
    return lax.ppermute(block, ("tm", "space"), route)


def away_side(block):
    return trade(block, [(TOUR[i], TOUR[i + 1]) for i in range(0, SLABS, 2)])


def chip_side(block):
    return trade(block, [(TOUR[i], TOUR[(i + 1) % SLABS]) for i in range(1, SLABS, 2)])


def off_chip(plane):
    return trade(plane, [(i, i + 1) for i in range(1, SLABS - 1, 2)], (0, SLABS - 1))


def on_chip(plane):
    return trade(plane, [(i, i + 1) for i in range(0, SLABS, 2)])


def call(kernel, out_shapes, args, specs, scratch=(), aliases=None, cost=None):
    return pl.pallas_call(
        kernel,
        out_shape=out_shapes,
        in_specs=specs,
        out_specs=jax.tree.map(lambda _: VM, out_shapes),
        scratch_shapes=list(scratch),
        input_output_aliases=aliases or {},
        cost_estimate=cost,
        compiler_params=pltpu.CompilerParams(vmem_limit_bytes=16 << 20),
    )(*args)


def f32(*shape):
    return jax.ShapeDtypeStruct(shape, jnp.float32)


def halving(rows, cols):
    r = lax.broadcasted_iota(jnp.int32, (rows, cols), 0)
    c = lax.broadcasted_iota(jnp.int32, (rows, cols), 1)
    hit = c // 2 == r if rows < cols else r // 2 == c
    return jnp.where(hit, 1.0, 0.0).astype(jnp.bfloat16)


def dot(a, ones):
    total = None
    for _ in range(3):
        part = a.astype(jnp.bfloat16)
        a = a - part.astype(jnp.float32)
        term = jnp.dot(part, ones, preferred_element_type=jnp.float32)
        total = term if total is None else total + term
    return total


def restrict_planes(first, second, tall):
    ny, nz = first.shape
    tall[...] = dot(first[...] + second[...], halving(nz, nz // 2))
    half = ny // 2
    return (tall[pl.ds(0, half, stride=2), :] + tall[pl.ds(1, half, stride=2), :]) * 0.125


def update_plane(mid, lower, upper, before, speed, force, weight, out, reach=None):
    ny, nz = mid.shape
    lane = lax.broadcasted_iota(jnp.int32, (ROWS, nz), 1)
    row = lax.broadcasted_iota(jnp.int32, (ROWS, nz), 0)
    for r0 in range(0, ny, ROWS):
        here = slice(r0, r0 + ROWS)
        m = mid[here, :]
        if r0 == 0:
            up = jnp.where(row == 0, 0.0, pltpu.roll(m, 1, 0))
        else:
            up = mid[r0 - 1 : r0 - 1 + ROWS, :]
        if r0 + ROWS == ny:
            down = jnp.where(row == ROWS - 1, 0.0, pltpu.roll(m, ROWS - 1, 0))
        else:
            down = mid[r0 + 1 : r0 + 1 + ROWS, :]
        left = jnp.where(lane == 0, 0.0, pltpu.roll(m, 1, 1))
        right = jnp.where(lane == nz - 1, 0.0, pltpu.roll(m, nz - 1, 1))
        low = lower[here, :] if reach is None else lower[here, :] * reach
        if upper is not None:
            low = low + upper[here, :]
        beside = low + (up + down) + (left + right)
        out[here, :] = (
            2.0 * m - before[here, :] + speed[here, :] * (beside - 6.0 * m) + weight * force[here, :]
        )


def sampled_row(planes, info, cell):
    ny, nz = planes[0].shape
    x = cell // (ny * nz) - info[1] * len(planes)
    y = lax.rem(cell // nz, ny)
    z = lax.rem(cell, nz)
    q = jnp.where(info[0] == 1, len(planes) - 1 - x, x)
    lane = lax.broadcasted_iota(jnp.int32, (1, nz), 1)
    row = jnp.zeros((1, nz), jnp.float32)
    for k, plane in enumerate(planes):
        row = jnp.where((lane == z) & (q == k), plane[pl.ds(y, 1), :], row)
    return row


def first_kernel(info, states, off, on, sems):
    def fetch(near, far):
        copies = [
            pltpu.make_async_copy(states.at[0, near], off, sems.at[0]),
            pltpu.make_async_copy(states.at[0, far], on, sems.at[1]),
        ]
        for copy in copies:
            copy.start()
        for copy in copies:
            copy.wait()

    @pl.when(info[0] == 1)
    def _():
        fetch(3, 0)

    @pl.when(info[0] == 0)
    def _():
        fetch(0, 3)

    @pl.when(info[2] == 0)
    def _():
        off[...] = jnp.zeros_like(off)
        on[...] = jnp.zeros_like(on)


def prep_kernel(info, courant, misfit, states, ce, ci, fe, fi, e0, inner, b0, binner, sems):
    def spread(flip):
        q = (lambda k: 3 - k) if flip else (lambda k: k)
        moves = [(states.at[0, q(0)], e0), (courant.at[q(0)], ce), (misfit.at[q(0)], fe)]
        moves += [(states.at[1, q(0)], b0)]
        for k in range(3):
            moves += [(states.at[0, q(k + 1)], inner.at[k]), (states.at[1, q(k + 1)], binner.at[k])]
            moves += [(courant.at[q(k + 1)], ci.at[k]), (misfit.at[q(k + 1)], fi.at[k])]
        copies = [pltpu.make_async_copy(a, b, sems.at[i]) for i, (a, b) in enumerate(moves)]
        for copy in copies:
            copy.start()
        for copy in copies:
            copy.wait()

    @pl.when(info[0] == 1)
    def _():
        spread(True)

    @pl.when(info[0] == 0)
    def _():
        spread(False)

    @pl.when(info[2] == 0)
    def _():
        for ref in (e0, inner, b0, binner):
            ref[...] = jnp.zeros_like(ref)


def restrict_kernel(courant, states, rb, rc, tall):
    block = rc.shape[2]
    for xc in range(2):
        r = restrict_planes(courant.at[2 * xc], courant.at[2 * xc + 1], tall)
        for s in range(SLABS):
            rc[s, xc] = r[PLACE[s] * block : (PLACE[s] + 1) * block, :]
        for lev in range(2):
            rb[lev, xc] = restrict_planes(states.at[lev, 2 * xc], states.at[lev, 2 * xc + 1], tall)


def edge_kernel(level, weights, reach, e0, inner, b0, off, ce, fe, n0):
    weight = weights[level : level + 1, :]
    update_plane(e0, off, inner.at[0], b0, ce, fe, weight, n0, reach[...])


def inner_kernel(level, taken, info, cells, weights, e0, inner, before, on, ci, fi, samples, n1, out, out_samples, beside):
    weight = weights[level : level + 1, :]
    ny = e0.shape[0]

    def pair(k, carry):
        here = pl.ds(pl.multiple_of(k * ROWS, ROWS), ROWS)
        beside[0, here, :] = e0[here, :] + inner[1, here, :]
        beside[1, here, :] = inner[0, here, :] + inner[2, here, :]
        beside[2, here, :] = inner[1, here, :] + on[here, :]
        return carry

    lax.fori_loop(0, ny // ROWS, pair, 0)

    def plane(k, carry):
        update_plane(inner.at[k], beside.at[k], None, before.at[k], ci.at[k], fi.at[k], weight, out.at[k])
        return carry

    lax.fori_loop(0, 3, plane, 0)

    def copy(k, carry):
        here = pl.ds(pl.multiple_of(k * ROWS, ROWS), ROWS)
        n1[here, :] = out[2, here, :]
        return carry

    lax.fori_loop(0, ny // ROWS, copy, 0)
    out_samples[...] = samples[...]
    if taken is not None:
        planes = (e0, inner.at[0], inner.at[1], inner.at[2])
        out_samples[taken : taken + 1, :] = sampled_row(planes, info, cells[taken])


def leave_kernel(info, cells, e0, inner, b0, binner, samples, rb, rc, out, sums, tall):
    odd = info[0] == 1
    block = out.shape[2]
    for lev, (first, mid) in enumerate(((e0, inner), (b0, binner))):
        sums[0] = restrict_planes(first, mid.at[0], tall)
        sums[1] = restrict_planes(mid.at[1], mid.at[2], tall)
        for xc in range(2):
            r = jnp.where(odd, sums[1 - xc], sums[xc]) - rb[lev, xc]
            for s in range(SLABS):
                out[s, lev * 2 + xc] = r[PLACE[s] * block : (PLACE[s] + 1) * block, :]
    for s in range(SLABS):
        out[s, 5:7] = rc[s]
    row = sampled_row((e0, inner.at[0], inner.at[1], inner.at[2]), info, cells[0])
    count = samples.shape[0]
    at = lax.broadcasted_iota(jnp.int32, (count, 1), 0)
    values = jnp.where(at == 0, jnp.sum(row), jnp.sum(samples[...], axis=1, keepdims=True))
    lane = lax.broadcasted_iota(jnp.int32, (count, 128), 1)
    level = lax.broadcasted_iota(jnp.int32, (count, 128), 0)
    line = jnp.sum(jnp.where(lane == level, values, 0.0), axis=0, keepdims=True)
    for s in range(SLABS):
        out[s, 4] = jnp.broadcast_to(line, (block, 128))


def phi_kernel(has_add, flags, state, on, off, speed, son, soff, *rest):
    if has_add:
        add, out, a, b, c = rest
    else:
        out, a, b, c = rest
    odd = flags[0:1, :] > 0.5
    near = flags[1:2, :]
    nx = speed.shape[0] * speed.shape[1]
    block = speed.shape[2]
    tall, nz = 3 * block, 128
    zero = jnp.zeros((tall, nz), jnp.float32)
    a[0], a[nx + 1], b[0], b[nx + 1] = zero, zero, zero, zero

    def fill(target, mine, other, far):
        far = far.reshape(nx, block, nz)
        other = other.reshape(nx, block, nz) * near
        target(slice(0, block), jnp.where(odd, other, far))
        target(slice(block, 2 * block), mine.reshape(nx, block, nz))
        target(slice(2 * block, tall), jnp.where(odd, far, other))

    def to_a(rows, value):
        a[1 : nx + 1, rows, :] = value

    def to_b(rows, value):
        b[1 : nx + 1, rows, :] = value

    def to_c(rows, value):
        c[:, rows, :] = value

    fill(to_a, state[:, 0:2], on[:, 0:2], off[:, 0:2])
    fill(to_b, state[:, 2:4], on[:, 2:4], off[:, 2:4])
    fill(to_c, speed[...], son[...], soff[...])

    step_x = 4
    lane = lax.broadcasted_iota(jnp.int32, (step_x, tall, nz), 2)

    def turn(now, then):
        def some(k, carry):
            x0 = k * step_x
            m = now[pl.ds(x0 + 1, step_x)]
            beside = now[pl.ds(x0, step_x)] + now[pl.ds(x0 + 2, step_x)]
            beside = beside + pltpu.roll(m, 1, 1) + pltpu.roll(m, tall - 1, 1)
            beside = beside + jnp.where(lane == 0, 0.0, pltpu.roll(m, 1, 2))
            beside = beside + jnp.where(lane == nz - 1, 0.0, pltpu.roll(m, nz - 1, 2))
            then[pl.ds(x0 + 1, step_x)] = (
                2.0 * m - then[pl.ds(x0 + 1, step_x)] + c[pl.ds(x0, step_x)] * (beside - 6.0 * m)
            )
            return carry

        lax.fori_loop(0, nx // step_x, some, 0, unroll=UNROLL)

    def two(_, carry):
        turn(a, b)
        turn(b, a)
        return carry

    lax.fori_loop(0, COARSE // 2, two, 0)
    rows = slice(block, 2 * block)
    one = a[1 : nx + 1, rows, :].reshape(SLABS, 2, block, nz)
    other = b[1 : nx + 1, rows, :].reshape(SLABS, 2, block, nz)
    if has_add:
        one = one + add[:, 0:2]
        other = other + add[:, 2:4]
    out[:, 0:2] = one
    out[:, 2:4] = other


def arrive_kernel(coarse, states, out, tall):
    block = coarse.shape[2]
    nzc = tall.shape[1]
    for lev in range(2):
        for xc in range(2):
            for s in range(SLABS):
                piece = coarse[s, lev * 2 + xc]
                for row in (0, 1):
                    tall[pl.ds(2 * PLACE[s] * block + row, block, stride=2), :] = piece
            fine = dot(tall[...], halving(nzc, 2 * nzc))
            out[lev, 2 * xc] = states[lev, 2 * xc] + fine
            out[lev, 2 * xc + 1] = states[lev, 2 * xc + 1] + fine


def body(courant, misfit, wavelet, source_cells, boundary_states):
    steps = wavelet.shape[0]
    ny, nz = courant.shape[1:]
    nyc, nzc = ny // 2, nz // 2
    block = nyc // SLABS
    slab = lax.axis_index("space")
    tm = lax.axis_index("tm")
    states = boundary_states[0]
    odd = lax.rem(slab, 2)
    alive = (tm > 0).astype(jnp.int32)
    reach = ((slab > 0) & (slab < SLABS - 1)).astype(jnp.int32)
    creach = ((slab != TOUR[0]) & (slab != TOUR[-1])).astype(jnp.int32)
    info = jnp.stack([odd, slab, alive, reach, creach]).astype(jnp.int32)
    ring = [(i, (i + 1) % GROUPS) for i in range(GROUPS)]
    back = [(i, (i - 1) % GROUPS) for i in range(GROUPS)]

    plane = f32(ny, nz)
    in_hbm = [pltpu.with_memory_space_constraint(x, pltpu.HBM) for x in (courant, misfit, states)]
    first_off, first_on = call(
        first_kernel,
        (plane, plane),
        (info, in_hbm[2]),
        [SM, HB],
        scratch=[pltpu.SemaphoreType.DMA((2,))],
    )
    off = off_chip(first_off)
    on = on_chip(first_on)
    wave, marks, _ = lax.optimization_barrier((wavelet, source_cells, first_off))
    packed = lax.ppermute(jnp.stack([wave, marks.astype(jnp.float32)]), "tm", ring)
    weights = jnp.broadcast_to(packed[0][:, None], (steps, nz))
    cells = packed[1].astype(jnp.int32)

    ce, ci, fe, fi, e0, inner, b0, binner = call(
        prep_kernel,
        (plane, f32(3, ny, nz)) * 4,
        (info, *in_hbm),
        [SM, HB, HB, HB],
        scratch=[pltpu.SemaphoreType.DMA((16,))],
    )
    away = jnp.broadcast_to(reach.astype(jnp.float32), (1, nz))
    samples = jnp.zeros((steps, nz), jnp.float32)
    for turn in range(steps):
        level = steps - 1 - turn
        n0 = call(
            functools.partial(edge_kernel, level),
            plane,
            (weights, away, e0, inner, b0, off, ce, fe),
            [VM] * 8,
        )
        if turn < steps - 1:
            off = off_chip(n0)
        n1, ninner, samples = call(
            functools.partial(inner_kernel, level, level + 1 if turn else None),
            (plane, f32(3, ny, nz), f32(steps, nz)),
            (info, cells, weights, e0, inner, binner, on, ci, fi, samples),
            [SM, SM] + [VM] * 8,
            scratch=[pltpu.VMEM((3, ny, nz), jnp.float32)],
        )
        if turn == 2:
            gate = lax.optimization_barrier((courant, states, n0))
            rb, speed = call(
                restrict_kernel,
                (f32(2, 2, nyc, nzc), f32(SLABS, 2, block, nzc)),
                gate[:2],
                [VM, VM],
                scratch=[pltpu.VMEM((ny, nzc), jnp.float32)],
            )
            n1, rb, speed = lax.optimization_barrier((n1, rb, speed))
            rb = lax.ppermute(rb, "tm", ring)
        if turn < steps - 1:
            on = on_chip(n1)
        e0, inner, b0, binner = n0, ninner, e0, inner

    pieces = call(
        leave_kernel,
        f32(SLABS, 7, block, nzc),
        (info, cells, e0, inner, b0, binner, samples, rb, speed),
        [SM, SM] + [VM] * 7,
        scratch=[pltpu.VMEM((2, nyc, nzc), jnp.float32), pltpu.VMEM((ny, nzc), jnp.float32)],
    )
    pieces = lax.all_to_all(pieces, "space", 0, 0)
    pieces, speed = pieces[:, :5], pieces[:, 5:7]
    lane = (1, nzc)
    parity = jnp.broadcast_to(odd.astype(jnp.float32), lane)
    near = jnp.broadcast_to(creach.astype(jnp.float32), lane)

    flags = jnp.concatenate([parity, near], axis=0)

    def phi(state, add=None):
        sides = (away_side(state), chip_side(state))
        nx = SLABS * 2
        args = (flags, state, sides[1], sides[0], speed, son, soff)
        args = args + (() if add is None else (add,))
        return call(
            functools.partial(phi_kernel, add is not None),
            f32(SLABS, 4, block, nzc),
            args,
            [VM] * len(args),
            scratch=[pltpu.VMEM((nx + 2, 3 * block, nzc), jnp.float32)] * 2
            + [pltpu.VMEM((nx, 3 * block, nzc), jnp.float32)],
        )

    def later(state, distance, aligned):
        route = []
        for to in range(GROUPS):
            group = to if aligned else (to - 1) % GROUPS
            route.append(((group + distance + 1) % GROUPS, to))
        group = tm if aligned else lax.rem(tm + GROUPS - 1, GROUPS)
        return lax.ppermute(state, "tm", route) * (group + distance < GROUPS).astype(jnp.float32)

    soff = away_side(speed)
    son = chip_side(speed)
    moved = lax.ppermute(pieces, "tm", back)
    moved, son, soff = lax.optimization_barrier((moved, son, soff))
    gradient = jnp.sum(moved[:, 4, 0, :], axis=0)[:steps]
    moved, gradient = lax.optimization_barrier((moved, gradient))
    moved = moved[:, :4] * (lax.rem(tm + GROUPS - 1, GROUPS) + 1 < GROUPS).astype(jnp.float32)
    total = phi(moved, pieces[:, :4])
    moved = later(total, 2, False)
    total = phi(phi(moved), total)
    moved = later(total, 4, True)
    own = lax.ppermute(total, "tm", back)
    for turn in range(4):
        moved = phi(moved, own if turn == 3 else None)
        if turn == 1:
            moved, own = lax.optimization_barrier((moved, own))
    coarse = lax.all_to_all(moved, "space", 0, 0)
    updated = call(
        arrive_kernel,
        f32(2, 4, ny, nz),
        (coarse, states),
        [VM, VM],
        scratch=[pltpu.VMEM((ny, nzc), jnp.float32)],
    )
    return (updated[None], gradient)


def solution(mesh):
    placed = (
        P("space", None, None),
        P("space", None, None),
        P("tm"),
        P("tm"),
        P("tm", None, "space", None, None),
    )

    return jax.shard_map(
        body,
        mesh=mesh,
        in_specs=placed,
        out_specs=(P("tm", None, "space", None, None), P("tm")),
        check_vma=False,
    )
```
